512 devices in a mesh: dp: 64 (over y, x, z_lo), mp: 8 (over z_hi, core).
Axes of the slice: x: 4, y: 4, z: 16 (z_hi: 4, z_lo: 4; z = z_hi * 4 + z_lo), core: 2. Of those that a mesh axis runs over, the one named last changes fastest.
Arguments:
- normed: bfloat16 [4096, 6144], P('mp', 'dp'), may hold values from -6 to 6
- hidden_cot: bfloat16 [4096, 12288], P('mp', 'dp'), may hold values from -6 to 6
- up_rows: bfloat16 [12288, 6144], P('dp'), may hold values from -0.078125 to 0.078125
Outputs:
- hidden: bfloat16 [4096, 12288], P('mp', 'dp')
- input_grad: bfloat16 [4096, 6144], P('mp', 'dp')
- up_grad: bfloat16 [12288, 6144], P('dp')
The draws below stay inside these ranges and needn't reach their ends.
All inputs are finite; a program needn't handle non-finite values.
Results may differ from the reference program's by a relative error of at most 0.013.
Values may be sent and summed in bfloat16 or wider, within the bound.
No kernel may reach another device: no remote copies, remote signals or barrier semaphores. Data moves between devices by JAX's collectives and lax.ppermute only.
A program may use at most 64 MiB of HBM per device.

```python
import jax
import jax.numpy as jnp
from jax import lax

D = 6144
TOK_DEV = 512
HID = 12288
TOKENS = 4096
REPLICAS = 8
N_MP = 8


def block_scale(stream_key, dims, shards, smallest, top_value):
    def one(axis_at, blocks):
        steps = jax.random.uniform(jax.random.fold_in(jax.random.fold_in(stream_key, 6), axis_at), (blocks,), jnp.float32, smallest / len(shards), top_value / len(shards))
        return jnp.repeat(jnp.exp(steps), dims[axis_at] // blocks).reshape((-1,) + (1,) * (len(dims) - axis_at - 1))

    loudness = one(*shards[0])
    for cut in shards[1:]:
        loudness = loudness * one(*cut)
    return loudness


def normal_values(stream_key, shape, width, limit, pieces=(), held_as=jnp.bfloat16):
    loudness = block_scale(stream_key, shape, pieces, -0.22, 0.18) if pieces else 1.0
    array = jax.random.normal(stream_key, shape, jnp.float32) * width * loudness
    return jnp.minimum(jnp.maximum(array, -limit), limit).astype(held_as)


def setup_inputs(seed: int = 0) -> dict:
    keys = jax.random.split(jax.random.key(seed), 4)
    normed = normal_values(keys[0], (TOKENS, D), 1.0, 6.0, ((0, 8), (1, 64)))
    hidden_cot = normal_values(keys[1], (TOKENS, HID), 1.0, 6.0, ((0, 8), (1, 64)))
    up_rows = normal_values(keys[2], (HID, D), D ** -0.5, 0.078125, ((0, 64),))
    return {"normed": normed, "hidden_cot": hidden_cot, "up_rows": up_rows}


inv_sqrt_two = 0.7071067811865476
inv_sqrt_two_pi = 0.3989422804014327

def gelu_parts(preact):
    normal_cdf = 0.5 * (1.0 + lax.erf(preact * inv_sqrt_two))
    gelu_out = preact * normal_cdf
    gelu_slope = normal_cdf + preact * jnp.exp(-0.5 * preact * preact) * inv_sqrt_two_pi
    return (gelu_out, gelu_slope)

def reference(normed, hidden_cot, up_rows):
    preact = jnp.dot(normed, up_rows.T, preferred_element_type=jnp.float32)
    gelu_out, gelu_slope = gelu_parts(preact)
    hidden = gelu_out.astype(jnp.bfloat16)
    hidden_grad = (hidden_cot.astype(jnp.float32) * gelu_slope).astype(jnp.bfloat16)
    grad_total = jnp.zeros(up_rows.shape, jnp.float32)
    for group in range(N_MP):
        lower = group * TOK_DEV
        group_term = jnp.dot(hidden_grad[lower:lower + TOK_DEV, :].T, normed[lower:lower + TOK_DEV, :], preferred_element_type=jnp.float32)
        rounded = lax.optimization_barrier(group_term.astype(jnp.bfloat16))
        grad_total = grad_total + rounded.astype(jnp.float32)
    up_grad = (grad_total / REPLICAS).astype(jnp.bfloat16)
    input_grad = jnp.dot(hidden_grad, up_rows, preferred_element_type=jnp.float32).astype(jnp.bfloat16)
    return (hidden, input_grad, up_grad)
```

```python
import jax
import jax.numpy as jnp
from jax import lax
from jax.experimental import pallas as pl
from jax.experimental.pallas import tpu as pltpu
from jax.sharding import Mesh
from jax.sharding import PartitionSpec as P

inv_sqrt_two = 0.7071067811865476
inv_sqrt_two_pi = 0.3989422804014327


RING = 4
F32 = jnp.float32
BF16 = jnp.bfloat16


def gelu_parts(preact):
    normal_cdf = 0.5 * (1.0 + lax.erf(preact * inv_sqrt_two))
    gelu_out = preact * normal_cdf
    gelu_slope = normal_cdf + preact * jnp.exp(-0.5 * preact * preact) * inv_sqrt_two_pi
    return (gelu_out, gelu_slope)


def shift(value, axis, by):
    size = lax.axis_size(axis)
    return lax.ppermute(value, axis, [(i, (i + by) % size) for i in range(size)])


def dot(left, right, dims):
    return lax.dot_general(left, right, (dims, ((), ())), preferred_element_type=F32)


def column_of(pos_ref, dy, dx, width):
    y = lax.rem(pos_ref[0] + dy, RING)
    x = lax.rem(pos_ref[1] + dx, RING)
    return pl.multiple_of((y * RING + x) * width, 128)


def forward_kernel(pos_ref, *refs):
    first, second = refs[0:4], refs[4:8]
    cot_ref, up_ref, hidden_ref, grad_ref, keep_ref, send_ref = refs[8:]
    width = up_ref.shape[1] // (RING * RING)
    half = first[0].shape[1]
    rows = keep_ref.shape[0]
    totals = [jnp.zeros((up_ref.shape[0], half), F32) for _ in range(2)]
    for dy in range(RING):
        for dx in range(RING):
            weights = up_ref[:, pl.ds(column_of(pos_ref, dy, dx, width), width)]
            totals[0] += dot(weights, first[dy][pl.ds(dx * width, width), :], ((1,), (0,)))
            totals[1] += dot(weights, second[dx][pl.ds(dy * width, width), :], ((1,), (0,)))
    for part, total in enumerate(totals):
        where = pl.ds(part * half, half)
        gelu_out, gelu_slope = gelu_parts(total)
        hidden_ref[:, where] = gelu_out.astype(BF16)
        grad_ref[:, where] = (cot_ref[:, where].astype(F32) * gelu_slope).astype(BF16)
    core = pos_ref[2]
    kept = grad_ref[pl.ds(pl.multiple_of(core * rows, 16), rows), :]
    sent = grad_ref[pl.ds(pl.multiple_of((1 - core) * rows, 16), rows), :]
    for dy in range(RING):
        for dx in range(RING):
            where = pl.ds(column_of(pos_ref, dy, dx, width), width)
            left = first[dy][pl.ds(dx * width, width), :]
            right = second[dx][pl.ds(dy * width, width), :]
            for grads, out_ref in ((sent, send_ref), (kept, keep_ref)):
                term = dot(grads[:, :half], left, ((1,), (1,)))
                term += dot(grads[:, half:], right, ((1,), (1,)))
                out_ref[:, where] = term.astype(BF16)


def input_grad_kernel(pos_ref, grad_ref, up_ref, *outs):
    first, second = outs[0:4], outs[4:8]
    width = up_ref.shape[1] // (RING * RING)
    half = first[0].shape[1]
    grads = grad_ref[...]
    for dy in range(RING):
        for dx in range(RING):
            weights = up_ref[:, pl.ds(column_of(pos_ref, dy, dx, width), width)]
            term = dot(weights, grads, ((0,), (0,))).astype(BF16)
            first[dy][pl.ds(dx * width, width), :] = term[:, :half]
            second[dx][pl.ds(dy * width, width), :] = term[:, half:]


def vmem(count):
    return [pl.BlockSpec(memory_space=pltpu.VMEM)] * count


def gather(value, axis):
    return [value] + [shift(value, axis, -d) for d in range(1, RING)]


def scatter_sum(values, axis):
    total = values[0].astype(F32)
    for d in range(1, RING):
        total = total + shift(values[d], axis, d).astype(F32)
    return total


def local(normed, hidden_cot, up_rows):
    y, x, zl, zh, core = (lax.axis_index(a) for a in ("y", "x", "zl", "zh", "c"))
    pos = jnp.stack([y, x, core]).astype(jnp.int32)
    hid, width = up_rows.shape
    tokens = normed.shape[0]
    half = tokens // 2

    block = lax.all_gather(normed.T, "zl", axis=0, tiled=True)
    first = gather(jnp.concatenate(gather(block[:, :half], "x"), axis=0), "y")
    second = gather(jnp.concatenate(gather(block[:, half:], "y"), axis=0), "x")

    hidden, hidden_grad, keep, send = pl.pallas_call(
        forward_kernel,
        in_specs=[pl.BlockSpec(memory_space=pltpu.SMEM)] + vmem(10),
        out_specs=vmem(4),
        out_shape=[jax.ShapeDtypeStruct((hid, tokens), BF16)] * 2
        + [jax.ShapeDtypeStruct((hid // 2, width), BF16)] * 2,
        name="forward",
        cost_estimate=pl.CostEstimate(
            flops=4 * hid * tokens * width, bytes_accessed=14_000_000, transcendentals=hid * tokens * 2
        ),
    )(pos, *first, *second, hidden_cot.T, up_rows)

    summed = (keep.astype(F32) + shift(send, "c", 1).astype(F32)).astype(BF16)
    rows = summed.shape[0] // RING
    cols = width // 2
    chunks = [
        lax.dynamic_slice_in_dim(summed, ((zh + d) % RING) * rows, rows, axis=0) for d in range(RING)
    ]
    left_half = shift(chunks[2][:, :cols], "zh", 1)
    right_half = shift(chunks[2][:, cols:], "zh", -1)
    ahead = jnp.concatenate(
        [(chunks[1][:, :cols].astype(F32) + left_half.astype(F32)).astype(BF16), chunks[1][:, cols:]], axis=1
    )
    behind = jnp.concatenate(
        [chunks[3][:, :cols], (chunks[3][:, cols:].astype(F32) + right_half.astype(F32)).astype(BF16)], axis=1
    )
    total = chunks[0].astype(F32) + shift(ahead, "zh", 1).astype(F32) + shift(behind, "zh", -1).astype(F32)

    parts = pl.pallas_call(
        input_grad_kernel,
        in_specs=[pl.BlockSpec(memory_space=pltpu.SMEM)] + vmem(2),
        out_specs=vmem(8),
        out_shape=[jax.ShapeDtypeStruct((width // RING, half), BF16)] * 8,
        name="input_grad",
        cost_estimate=pl.CostEstimate(
            flops=2 * hid * tokens * width, bytes_accessed=9_000_000, transcendentals=0
        ),
    )(pos, hidden_grad, up_rows)
    sums = []
    for pieces, axes in ((parts[:4], ("y", "x")), (parts[4:], ("x", "y"))):
        stage = scatter_sum(pieces, axes[0]).astype(BF16)
        depth = stage.shape[0] // RING
        sums.append(scatter_sum([stage[d * depth : (d + 1) * depth] for d in range(RING)], axes[1]).astype(BF16))
    stage = jnp.concatenate(sums, axis=1)
    depth = stage.shape[0] // RING
    input_grad = scatter_sum(
        [lax.dynamic_slice_in_dim(stage, ((zl + d) % RING) * depth, depth, axis=0) for d in range(RING)], "zl"
    ).astype(BF16)

    mine = (total / (2 * RING)).astype(BF16)
    before = shift(mine, "zh", 1)
    after = shift(mine, "zh", -1)
    across = jnp.concatenate([shift(before[:, :cols], "zh", 1), shift(after[:, cols:], "zh", -1)], axis=1)
    ring = jnp.concatenate([mine, after, across, before], axis=0)
    ring = jnp.concatenate([ring, ring], axis=0)
    own = lax.dynamic_slice_in_dim(ring, ((RING - zh) % RING) * rows, RING * rows, axis=0)
    other = shift(own, "c", 1)
    up_grad = jnp.where(
        core == 0, jnp.concatenate([own, other], axis=0), jnp.concatenate([other, own], axis=0)
    )
    return (hidden.T, input_grad.T, up_grad)


def solution(mesh):
    inner = Mesh(mesh.devices.reshape(RING, RING, RING, RING, 2), ("y", "x", "zl", "zh", "c"))
    tokens, features = ("zh", "c"), ("y", "x", "zl")
    return jax.shard_map(
        local,
        mesh=inner,
        in_specs=(P(tokens, features), P(tokens, features), P(features, None)),
        out_specs=(P(tokens, features), P(tokens, features), P(features, None)),
        check_vma=False,
    )
```

```python
import jax
import jax.numpy as jnp
from jax import lax
from jax.experimental import pallas as pl
from jax.experimental.pallas import tpu as pltpu
from jax.sharding import Mesh
from jax.sharding import PartitionSpec as P


inv_sqrt_two = 0.7071067811865476
inv_sqrt_two_pi = 0.3989422804014327


RING = 4
F32 = jnp.float32
BF16 = jnp.bfloat16


def gelu_parts(preact):
    normal_cdf = 0.5 * (1.0 + lax.erf(preact * inv_sqrt_two))
    gelu_out = preact * normal_cdf
    gelu_slope = normal_cdf + preact * jnp.exp(-0.5 * preact * preact) * inv_sqrt_two_pi
    return (gelu_out, gelu_slope)


def shift(value, axis, by):
    size = lax.axis_size(axis)
    return lax.ppermute(value, axis, [(i, (i + by) % size) for i in range(size)])


def dot(left, right, dims):
    return lax.dot_general(left, right, (dims, ((), ())), preferred_element_type=F32)


def column_of(pos_ref, outer, inner, width):
    core = pos_ref[2]
    dy = outer + core * (inner - outer)
    dx = inner + core * (outer - inner)
    y = lax.rem(pos_ref[0] + dy, RING)
    x = lax.rem(pos_ref[1] + dx, RING)
    return pl.multiple_of((y * RING + x) * width, 128)


def order_kernel(pos_ref, up_ref, out_ref):
    width = up_ref.shape[1] // (RING * RING)
    for outer in range(RING):
        for inner in range(RING):
            out_ref[:, pl.ds((outer * RING + inner) * width, width)] = up_ref[
                :, pl.ds(column_of(pos_ref, outer, inner, width), width)
            ]


def forward_kernel(pos_ref, *refs):
    pieces = refs[0:RING]
    cot_ref, up_ref, hidden_ref, grad_ref, keep_ref, send_ref = refs[RING:]
    depth = pieces[0].shape[0]
    width = depth // RING
    rows = keep_ref.shape[0]
    total = dot(up_ref[:, pl.ds(0, depth)], pieces[0][...], ((1,), (0,)))
    for d in range(1, RING):
        total += dot(up_ref[:, pl.ds(d * depth, depth)], pieces[d][...], ((1,), (0,)))
    gelu_out, gelu_slope = gelu_parts(total)
    hidden_ref[...] = gelu_out.astype(BF16)
    grad_ref[...] = (cot_ref[...].astype(F32) * gelu_slope).astype(BF16)
    core, zh = pos_ref[2], pos_ref[3]
    for half, out_ref in ((1 - core, send_ref), (core, keep_ref)):
        grads = grad_ref[pl.ds(pl.multiple_of(half * rows, 16), rows), :]
        for d in range(RING):
            term = dot(grads, pieces[d][...], ((1,), (1,))).astype(BF16)
            for inner in range(RING):
                column = column_of(pos_ref, d, inner, width) + (RING - zh) * depth
                column = pl.multiple_of(lax.rem(column, RING * depth), 128)
                out_ref[:, pl.ds(column, width)] = term[:, inner * width : (inner + 1) * width]


def input_grad_kernel(grad_ref, up_ref, *outs):
    grads = grad_ref[...]
    depth = outs[0].shape[0]
    for d in range(RING):
        term = dot(up_ref[:, pl.ds(d * depth, depth)], grads, ((0,), (0,)))
        outs[d][...] = term.astype(BF16)


def place_kernel(pos_ref, own_ref, own_last_ref, other_ref, other_last_ref, out_ref):
    core, zh = pos_ref[2], pos_ref[3]
    rows, depth = own_last_ref.shape
    for half, most, last in ((core, own_ref, own_last_ref), (1 - core, other_ref, other_last_ref)):
        where = pl.ds(pl.multiple_of(half * rows, 16), rows)
        for d, (ref, at) in enumerate(((most, 0), (most, 1), (last, 0), (most, 2))):
            column = pl.multiple_of(lax.rem(zh + d, RING) * depth, 128)
            out_ref[where, pl.ds(column, depth)] = ref[:, at * depth : (at + 1) * depth]


def vmem(count):
    return [pl.BlockSpec(memory_space=pltpu.VMEM)] * count


def turn(value, late, by):
    def target(y, x, c):
        if (c == 0) != late:
            return (y, (x + by) % RING, c)
        return ((y + by) % RING, x, c)

    def flat(y, x, c):
        return (y * RING + x) * 2 + c

    spots = [(y, x, c) for y in range(RING) for x in range(RING) for c in range(2)]
    return lax.ppermute(value, ("y", "x", "c"), [(flat(*s), flat(*target(*s))) for s in spots])


def gather(value, late):
    return [value] + [turn(value, late, -d) for d in range(1, RING)]


def add_up(values):
    total = values[0].astype(F32)
    for value in values[1:]:
        total = total + value.astype(F32)
    return total


def scatter_sum(values, late):
    return add_up([values[0]] + [turn(values[d], late, d) for d in range(1, RING)])


def work(normed, hidden_cot, up_rows):
    y, x, zl, zh, core = (lax.axis_index(a) for a in ("y", "x", "zl", "zh", "c"))
    pos = jnp.stack([y, x, core, zh]).astype(jnp.int32)
    hid, width = up_rows.shape
    tokens = normed.shape[0]
    scalars = pl.BlockSpec(memory_space=pltpu.SMEM)

    ordered = pl.pallas_call(
        order_kernel,
        in_specs=[scalars] + vmem(1),
        out_specs=vmem(1)[0],
        out_shape=jax.ShapeDtypeStruct((hid, width), BF16),
        name="order",
        cost_estimate=pl.CostEstimate(flops=0, bytes_accessed=4 * hid * width, transcendentals=0),
    )(pos, up_rows)

    block = lax.all_gather(normed.T, "zl", axis=0, tiled=True)
    pieces = gather(jnp.concatenate(gather(block, False), axis=0), True)

    hidden, hidden_grad, keep, send = pl.pallas_call(
        forward_kernel,
        in_specs=[scalars] + vmem(RING + 2),
        out_specs=vmem(4),
        out_shape=[jax.ShapeDtypeStruct((hid, tokens), BF16)] * 2
        + [jax.ShapeDtypeStruct((hid // 2, width), BF16)] * 2,
        name="forward",
        cost_estimate=pl.CostEstimate(
            flops=4 * hid * tokens * width, bytes_accessed=14_000_000, transcendentals=hid * tokens * 2
        ),
    )(pos, *pieces, hidden_cot.T, ordered)

    depth = width // RING
    rows = hid // 2
    arrived = shift(send, "c", 1)
    quarters = [
        (keep[:, d * depth : (d + 1) * depth].astype(F32) + arrived[:, d * depth : (d + 1) * depth].astype(F32)).astype(BF16)
        for d in range(RING)
    ]
    upper = shift(quarters[2][: rows // 2], "zh", 1)
    lower = shift(quarters[2][rows // 2 :], "zh", -1)
    ahead = jnp.concatenate([add_up([quarters[1][: rows // 2], upper]).astype(BF16), quarters[1][rows // 2 :]], axis=0)
    behind = jnp.concatenate([quarters[3][: rows // 2], add_up([quarters[3][rows // 2 :], lower]).astype(BF16)], axis=0)
    arrived = [shift(ahead, "zh", 1), shift(behind, "zh", -1)]
    mine = (add_up([quarters[0]] + arrived) / (2 * RING)).astype(BF16)
    before = shift(mine, "zh", 1)
    after = shift(mine, "zh", -1)
    across = [shift(before[: rows // 2], "zh", 1), shift(after[rows // 2 :], "zh", -1)]
    most = jnp.concatenate([mine, after, before], axis=1)
    last = jnp.concatenate(across, axis=0)
    other_most = shift(most, "c", 1)
    other_last = shift(last, "c", 1)
    up_grad = pl.pallas_call(
        place_kernel,
        in_specs=[scalars] + vmem(4),
        out_specs=vmem(1)[0],
        out_shape=jax.ShapeDtypeStruct((hid, width), BF16),
        name="place",
        cost_estimate=pl.CostEstimate(flops=0, bytes_accessed=4 * hid * width, transcendentals=0),
    )(pos, most, last, other_most, other_last)

    parts = pl.pallas_call(
        input_grad_kernel,
        in_specs=vmem(2),
        out_specs=vmem(RING),
        out_shape=[jax.ShapeDtypeStruct((width // RING, tokens), BF16)] * RING,
        name="partial",
        cost_estimate=pl.CostEstimate(
            flops=2 * hid * tokens * width, bytes_accessed=9_000_000, transcendentals=0
        ),
    )(hidden_grad, ordered)
    stage = scatter_sum(parts, True).astype(BF16)
    depth = stage.shape[0] // RING
    stage = scatter_sum([stage[d * depth : (d + 1) * depth] for d in range(RING)], False).astype(BF16)
    depth = stage.shape[0] // RING
    shares = [lax.dynamic_slice_in_dim(stage, ((zl + d) % RING) * depth, depth, axis=0) for d in range(RING)]
    input_grad = add_up(shares[:1] + [shift(shares[d], "zl", d) for d in range(1, RING)]).astype(BF16)
    return (hidden.T, input_grad.T, up_grad)


def solution(mesh):
    inner = Mesh(mesh.devices.reshape(RING, RING, RING, RING, 2), ("y", "x", "zl", "zh", "c"))
    tokens, features = ("zh", "c"), ("y", "x", "zl")
    return jax.shard_map(
        work,
        mesh=inner,
        in_specs=(P(tokens, features), P(tokens, features), P(features, None)),
        out_specs=(P(tokens, features), P(tokens, features), P(features, None)),
        check_vma=False,
    )
```

```python
import jax
import jax.numpy as jnp
from jax import lax
from jax.experimental import pallas as pl
from jax.experimental.pallas import tpu as pltpu
from jax.sharding import Mesh
from jax.sharding import PartitionSpec as P


inv_sqrt_two = 0.7071067811865476
inv_sqrt_two_pi = 0.3989422804014327


RING = 4
F32 = jnp.float32
BF16 = jnp.bfloat16


def gelu_parts(preact):
    normal_cdf = 0.5 * (1.0 + lax.erf(preact * inv_sqrt_two))
    gelu_out = preact * normal_cdf
    gelu_slope = normal_cdf + preact * jnp.exp(-0.5 * preact * preact) * inv_sqrt_two_pi
    return (gelu_out, gelu_slope)


def shift(value, axis, by):
    size = lax.axis_size(axis)
    return lax.ppermute(value, axis, [(i, (i + by) % size) for i in range(size)])


def dot(left, right, dims):
    return lax.dot_general(left, right, (dims, ((), ())), preferred_element_type=F32)


def column_of(pos_ref, outer, inner, width):
    core = pos_ref[2]
    dy = outer + core * (inner - outer)
    dx = inner + core * (outer - inner)
    y = lax.rem(pos_ref[0] + dy, RING)
    x = lax.rem(pos_ref[1] + dx, RING)
    return pl.multiple_of((y * RING + x) * width, 128)


def order_kernel(pos_ref, up_ref, out_ref):
    width = up_ref.shape[1] // (RING * RING)
    for outer in range(RING):
        for inner in range(RING):
            out_ref[:, pl.ds((outer * RING + inner) * width, width)] = up_ref[
                :, pl.ds(column_of(pos_ref, outer, inner, width), width)
            ]


def early_kernel(up_ref, *refs):
    total_ref = refs[-1]
    depth = refs[0].shape[0]
    total = None
    for place, ref in zip((0, 1, 2, 3, 6, 7), refs[:-1]):
        term = dot(up_ref[:, pl.ds(place * depth, depth)], ref[...], ((1,), (0,)))
        total = term if total is None else total + term
    total_ref[...] = total


def forward_kernel(pos_ref, *refs):
    pieces = refs[0 : 2 * RING]
    early_ref, cot_ref, up_ref, hidden_ref, grad_ref, keep_ref, send_ref, packed_ref = refs[2 * RING :]
    depth = pieces[0].shape[0]
    width = depth // 2
    rows = keep_ref.shape[0]
    total = early_ref[...]
    for place in (4, 5):
        total += dot(up_ref[:, pl.ds(place * depth, depth)], pieces[place][...], ((1,), (0,)))
    gelu_out, gelu_slope = gelu_parts(total)
    hidden_ref[...] = gelu_out.astype(BF16)
    grad_ref[...] = (cot_ref[...].astype(F32) * gelu_slope).astype(BF16)
    core, zh = pos_ref[2], pos_ref[3]
    for at, half in enumerate((1 - core, core)):
        packed_ref[pl.ds(at * rows, rows), :] = grad_ref[pl.ds(pl.multiple_of(half * rows, 16), rows), :]
    grads = packed_ref[...]
    for place, piece in enumerate(pieces):
        term = dot(grads, piece[...], ((1,), (1,))).astype(BF16)
        for part in range(2):
            block = 2 * place + part
            column = column_of(pos_ref, block // RING, block % RING, width) + (RING - zh) * 2 * depth
            column = pl.multiple_of(lax.rem(column, 2 * RING * depth), 128)
            send_ref[:, pl.ds(column, width)] = term[:rows, part * width : (part + 1) * width]
            keep_ref[:, pl.ds(column, width)] = term[rows:, part * width : (part + 1) * width]


def input_grad_kernel(grad_ref, up_ref, *outs):
    grads = grad_ref[...]
    depth = outs[0].shape[0]
    for d in range(RING):
        term = dot(up_ref[:, pl.ds(d * depth, depth)], grads, ((0,), (0,)))
        outs[d][...] = term.astype(BF16)


def place_kernel(pos_ref, *refs):
    core, zh = pos_ref[2], pos_ref[3]
    out_ref = refs[-1]
    rows, depth = refs[0].shape
    for half, (mine, near, far) in ((core, refs[0:3]), (1 - core, refs[3:6])):
        where = pl.ds(pl.multiple_of(half * rows, 16), rows)
        for d, ref, at in ((0, mine, 0), (1, near, 0), (3, near, 1), (2, far, 0)):
            column = pl.multiple_of(lax.rem(zh + d, RING) * depth, 128)
            out_ref[where, pl.ds(column, depth)] = ref[:, at * depth : (at + 1) * depth]


def vmem(count):
    return [pl.BlockSpec(memory_space=pltpu.VMEM)] * count


def turn(value, late, by):
    def target(y, x, c):
        if (c == 0) != late:
            return (y, (x + by) % RING, c)
        return ((y + by) % RING, x, c)

    def flat(y, x, c):
        return (y * RING + x) * 2 + c

    spots = [(y, x, c) for y in range(RING) for x in range(RING) for c in range(2)]
    return lax.ppermute(value, ("y", "x", "c"), [(flat(*s), flat(*target(*s))) for s in spots])


def gather(value, late):
    return [value] + [turn(value, late, -d) for d in range(1, RING)]


def add_up(values):
    total = values[0].astype(F32)
    for value in values[1:]:
        total = total + value.astype(F32)
    return total


def scatter_sum(values, late):
    return add_up([values[0]] + [turn(values[d], late, d) for d in range(1, RING)])


def work(normed, hidden_cot, up_rows):
    y, x, zl, zh, core = (lax.axis_index(a) for a in ("y", "x", "zl", "zh", "c"))
    pos = jnp.stack([y, x, core, zh]).astype(jnp.int32)
    hid, width = up_rows.shape
    tokens = normed.shape[0]
    scalars = pl.BlockSpec(memory_space=pltpu.SMEM)

    ordered = pl.pallas_call(
        order_kernel,
        in_specs=[scalars] + vmem(1),
        out_specs=vmem(1)[0],
        out_shape=jax.ShapeDtypeStruct((hid, width), BF16),
        name="order",
        cost_estimate=pl.CostEstimate(flops=0, bytes_accessed=4 * hid * width, transcendentals=0),
    )(pos, up_rows)

    block = lax.all_gather(normed.T, "zl", axis=0, tiled=True)
    quarters = gather(block, False)
    upper, lower = jnp.concatenate(quarters[:2], axis=0), jnp.concatenate(quarters[2:], axis=0)
    upper1, lower3 = turn(upper, True, -1), turn(lower, True, 1)
    lower1, upper3 = turn(lower, True, -1), turn(upper, True, 1)
    upper2, lower2 = turn(upper1, True, -1), turn(lower3, True, 1)
    pieces = [upper, lower, upper1, lower1, upper2, lower2, upper3, lower3]
    early = pl.pallas_call(
        early_kernel,
        in_specs=vmem(7),
        out_specs=vmem(1)[0],
        out_shape=jax.ShapeDtypeStruct((hid, tokens), F32),
        name="early",
        cost_estimate=pl.CostEstimate(flops=3 * hid * tokens * width // 2, bytes_accessed=7_000_000, transcendentals=0),
    )(ordered, *pieces[:4], *pieces[6:])

    hidden, hidden_grad, keep, send = pl.pallas_call(
        forward_kernel,
        in_specs=[scalars] + vmem(2 * RING + 3),
        out_specs=vmem(4),
        out_shape=[jax.ShapeDtypeStruct((hid, tokens), BF16)] * 2
        + [jax.ShapeDtypeStruct((hid // 2, width), BF16)] * 2,
        scratch_shapes=[pltpu.VMEM((hid, tokens), BF16)],
        name="forward",
        cost_estimate=pl.CostEstimate(
            flops=3 * hid * tokens * width, bytes_accessed=14_000_000, transcendentals=hid * tokens * 2
        ),
    )(pos, *pieces, early, hidden_cot.T, ordered)

    depth = width // RING
    arrived = shift(send, "c", 1)
    quarters = [
        add_up([keep[:, d * depth : (d + 1) * depth], arrived[:, d * depth : (d + 1) * depth]]).astype(BF16)
        for d in range(RING)
    ]
    arrived = [shift(quarters[2], "zh", 2)]
    arrived += [shift(quarters[1], "zh", 1), shift(quarters[3], "zh", -1)]
    mine = (add_up([quarters[0]] + arrived) / (2 * RING)).astype(BF16)
    far = shift(mine, "zh", 2)
    near = jnp.concatenate([shift(mine, "zh", -1), shift(mine, "zh", 1)], axis=1)
    other_mine = shift(mine, "c", 1)
    other_near = shift(near, "c", 1)
    other_far = shift(far, "c", 1)
    up_grad = pl.pallas_call(
        place_kernel,
        in_specs=[scalars] + vmem(6),
        out_specs=vmem(1)[0],
        out_shape=jax.ShapeDtypeStruct((hid, width), BF16),
        name="place",
        cost_estimate=pl.CostEstimate(flops=0, bytes_accessed=4 * hid * width, transcendentals=0),
    )(pos, mine, near, far, other_mine, other_near, other_far)

    parts = pl.pallas_call(
        input_grad_kernel,
        in_specs=vmem(2),
        out_specs=vmem(RING),
        out_shape=[jax.ShapeDtypeStruct((width // RING, tokens), BF16)] * RING,
        name="partial",
        cost_estimate=pl.CostEstimate(
            flops=2 * hid * tokens * width, bytes_accessed=9_000_000, transcendentals=0
        ),
    )(hidden_grad, ordered)
    stage = scatter_sum(parts, True).astype(BF16)
    depth = stage.shape[0] // RING
    stage = scatter_sum([stage[d * depth : (d + 1) * depth] for d in range(RING)], False).astype(BF16)
    depth = stage.shape[0] // RING
    shares = [lax.dynamic_slice_in_dim(stage, ((zl + d) % RING) * depth, depth, axis=0) for d in range(RING)]
    input_grad = add_up(shares[:1] + [shift(shares[d], "zl", d) for d in range(1, RING)]).astype(BF16)
    return (hidden.T, input_grad.T, up_grad)


def solution(mesh):
    inner = Mesh(mesh.devices.reshape(RING, RING, RING, RING, 2), ("y", "x", "zl", "zh", "c"))
    tokens, features = ("zh", "c"), ("y", "x", "zl")
    return jax.shard_map(
        work,
        mesh=inner,
        in_specs=(P(tokens, features), P(tokens, features), P(features, None)),
        out_specs=(P(tokens, features), P(tokens, features), P(features, None)),
        check_vma=False,
    )
```

```python
import jax
import jax.numpy as jnp
from jax import lax
from jax.experimental import pallas as pl
from jax.experimental.pallas import tpu as pltpu
from jax.sharding import Mesh
from jax.sharding import PartitionSpec as P


inv_sqrt_two = 0.7071067811865476
inv_sqrt_two_pi = 0.3989422804014327


RING = 4
F32 = jnp.float32
BF16 = jnp.bfloat16


def gelu_parts(preact):
    normal_cdf = 0.5 * (1.0 + lax.erf(preact * inv_sqrt_two))
    gelu_out = preact * normal_cdf
    gelu_slope = normal_cdf + preact * jnp.exp(-0.5 * preact * preact) * inv_sqrt_two_pi
    return (gelu_out, gelu_slope)


def shift(value, axis, by):
    size = lax.axis_size(axis)
    return lax.ppermute(value, axis, [(i, (i + by) % size) for i in range(size)])


def dot(left, right, dims):
    return lax.dot_general(left, right, (dims, ((), ())), preferred_element_type=F32)


def column_of(pos_ref, outer, inner, width):
    core = pos_ref[2]
    dy = outer + core * (inner - outer)
    dx = inner + core * (outer - inner)
    y = lax.rem(pos_ref[0] + dy, RING)
    x = lax.rem(pos_ref[1] + dx, RING)
    return pl.multiple_of((y * RING + x) * width, 128)


def order_kernel(pos_ref, up_ref, out_ref):
    width = up_ref.shape[1] // (RING * RING)
    for outer in range(RING):
        for inner in range(RING):
            out_ref[:, pl.ds((outer * RING + inner) * width, width)] = up_ref[
                :, pl.ds(column_of(pos_ref, outer, inner, width), width)
            ]


def early_kernel(up_ref, *refs):
    total_ref = refs[-1]
    depth = refs[0].shape[0]
    total = None
    for place, ref in zip((0, 1, 2, 3, 6, 7), refs[:-1]):
        term = dot(up_ref[:, pl.ds(place * depth, depth)], ref[...], ((1,), (0,)))
        total = term if total is None else total + term
    total_ref[...] = total


def forward_kernel(pos_ref, *refs):
    pieces = refs[0 : 2 * RING]
    early_ref, cot_ref, up_ref, hidden_ref, grad_ref, keep_ref, send_ref, packed_ref = refs[2 * RING :]
    depth = pieces[0].shape[0]
    width = depth // 2
    rows = keep_ref.shape[0]
    total = early_ref[...]
    for place in (4, 5):
        total += dot(up_ref[:, pl.ds(place * depth, depth)], pieces[place][...], ((1,), (0,)))
    gelu_out, gelu_slope = gelu_parts(total)
    hidden_ref[...] = gelu_out.astype(BF16)
    grad_ref[...] = (cot_ref[...].astype(F32) * gelu_slope).astype(BF16)
    core, zh = pos_ref[2], pos_ref[3]
    for at, half in enumerate((1 - core, core)):
        packed_ref[pl.ds(at * rows, rows), :] = grad_ref[pl.ds(pl.multiple_of(half * rows, 16), rows), :]
    grads = packed_ref[...]
    for place, piece in enumerate(pieces):
        term = dot(grads, piece[...], ((1,), (1,))).astype(BF16)
        for part in range(2):
            block = 2 * place + part
            column = column_of(pos_ref, block // RING, block % RING, width) + (RING - zh) * 2 * depth
            column = pl.multiple_of(lax.rem(column, 2 * RING * depth), 128)
            send_ref[:, pl.ds(column, width)] = term[:rows, part * width : (part + 1) * width]
            keep_ref[:, pl.ds(column, width)] = term[rows:, part * width : (part + 1) * width]


def input_grad_kernel(grad_ref, up_ref, *outs):
    grads = grad_ref[...]
    depth = outs[0].shape[0]
    for d in range(RING):
        term = dot(up_ref[:, pl.ds(d * depth, depth)], grads, ((0,), (0,)))
        outs[d][...] = term.astype(BF16)


def place_kernel(pos_ref, *refs):
    core, zh = pos_ref[2], pos_ref[3]
    out_ref = refs[-1]
    rows, depth = refs[0].shape
    for half, (mine, near, far) in ((core, refs[0:3]), (1 - core, refs[3:6])):
        where = pl.ds(pl.multiple_of(half * rows, 16), rows)
        for d, ref, at in ((0, mine, 0), (1, near, 0), (3, near, 1), (2, far, 0)):
            column = pl.multiple_of(lax.rem(zh + d, RING) * depth, 128)
            out_ref[where, pl.ds(column, depth)] = ref[:, at * depth : (at + 1) * depth]


def vmem(count):
    return [pl.BlockSpec(memory_space=pltpu.VMEM)] * count


def turn(value, late, by):
    def target(y, x, c):
        if (c == 0) != late:
            return (y, (x + by) % RING, c)
        return ((y + by) % RING, x, c)

    def flat(y, x, c):
        return (y * RING + x) * 2 + c

    spots = [(y, x, c) for y in range(RING) for x in range(RING) for c in range(2)]
    return lax.ppermute(value, ("y", "x", "c"), [(flat(*s), flat(*target(*s))) for s in spots])


def gather(value, late):
    return [value] + [turn(value, late, -d) for d in range(1, RING)]


def add_up(values):
    total = values[0].astype(F32)
    for value in values[1:]:
        total = total + value.astype(F32)
    return total


def scatter_sum(values, late):
    return add_up([values[0]] + [turn(values[d], late, d) for d in range(1, RING)])


def work(normed, hidden_cot, up_rows):
    y, x, zl, zh, core = (lax.axis_index(a) for a in ("y", "x", "zl", "zh", "c"))
    pos = jnp.stack([y, x, core, zh]).astype(jnp.int32)
    hid, width = up_rows.shape
    tokens = normed.shape[0]
    scalars = pl.BlockSpec(memory_space=pltpu.SMEM)

    ordered = pl.pallas_call(
        order_kernel,
        in_specs=[scalars] + vmem(1),
        out_specs=vmem(1)[0],
        out_shape=jax.ShapeDtypeStruct((hid, width), BF16),
        name="order",
        cost_estimate=pl.CostEstimate(flops=0, bytes_accessed=4 * hid * width, transcendentals=0),
    )(pos, up_rows)

    block = lax.all_gather(normed.T, "zl", axis=0, tiled=True)
    quarters = gather(block, False)
    upper, lower = jnp.concatenate(quarters[:2], axis=0), jnp.concatenate(quarters[2:], axis=0)
    upper1, lower3 = turn(upper, True, -1), turn(lower, True, 1)
    lower1, upper3 = turn(lower, True, -1), turn(upper, True, 1)
    upper2, lower2 = turn(upper1, True, -1), turn(lower3, True, 1)
    pieces = [upper, lower, upper1, lower1, upper2, lower2, upper3, lower3]
    early = pl.pallas_call(
        early_kernel,
        in_specs=vmem(7),
        out_specs=vmem(1)[0],
        out_shape=jax.ShapeDtypeStruct((hid, tokens), F32),
        name="early",
        cost_estimate=pl.CostEstimate(flops=3 * hid * tokens * width // 2, bytes_accessed=7_000_000, transcendentals=0),
    )(ordered, *pieces[:4], *pieces[6:])

    hidden, hidden_grad, keep, send = pl.pallas_call(
        forward_kernel,
        in_specs=[scalars] + vmem(2 * RING + 3),
        out_specs=vmem(4),
        out_shape=[jax.ShapeDtypeStruct((hid, tokens), BF16)] * 2
        + [jax.ShapeDtypeStruct((hid // 2, width), BF16)] * 2,
        scratch_shapes=[pltpu.VMEM((hid, tokens), BF16)],
        name="forward",
        cost_estimate=pl.CostEstimate(
            flops=3 * hid * tokens * width, bytes_accessed=14_000_000, transcendentals=hid * tokens * 2
        ),
    )(pos, *pieces, early, hidden_cot.T, ordered)

    depth = width // RING
    arrived = shift(send, "c", 1)
    quarters = [
        add_up([keep[:, d * depth : (d + 1) * depth], arrived[:, d * depth : (d + 1) * depth]]).astype(BF16)
        for d in range(RING)
    ]
    mid = quarters[0].shape[0] // 2
    upper = [quarter[:mid] for quarter in quarters]
    lower = [quarter[mid:] for quarter in quarters]
    upper_in, lower_in = shift(upper[2], "zh", 1), shift(lower[2], "zh", -1)
    lower_from_left, upper_from_right = shift(lower[1], "zh", 1), shift(upper[3], "zh", -1)
    upper_from_left = shift(add_up([upper[1], upper_in]).astype(BF16), "zh", 1)
    lower_from_right = shift(add_up([lower[3], lower_in]).astype(BF16), "zh", -1)
    upper0 = (add_up([upper[0], upper_from_left, upper_from_right]) / (2 * RING)).astype(BF16)
    lower0 = (add_up([lower[0], lower_from_left, lower_from_right]) / (2 * RING)).astype(BF16)
    upper1, lower3 = shift(upper0, "zh", -1), shift(lower0, "zh", 1)
    lower1, upper3 = shift(lower0, "zh", -1), shift(upper0, "zh", 1)
    upper2, lower2 = shift(upper1, "zh", -1), shift(lower3, "zh", 1)
    mine = jnp.concatenate([upper0, lower0], axis=0)
    near = jnp.concatenate(
        [jnp.concatenate([upper1, upper3], axis=1), jnp.concatenate([lower1, lower3], axis=1)], axis=0
    )
    far = jnp.concatenate([upper2, lower2], axis=0)
    other_mine = shift(mine, "c", 1)
    other_near = shift(near, "c", 1)
    other_far = shift(far, "c", 1)
    up_grad = pl.pallas_call(
        place_kernel,
        in_specs=[scalars] + vmem(6),
        out_specs=vmem(1)[0],
        out_shape=jax.ShapeDtypeStruct((hid, width), BF16),
        name="place",
        cost_estimate=pl.CostEstimate(flops=0, bytes_accessed=4 * hid * width, transcendentals=0),
    )(pos, mine, near, far, other_mine, other_near, other_far)

    parts = pl.pallas_call(
        input_grad_kernel,
        in_specs=vmem(2),
        out_specs=vmem(RING),
        out_shape=[jax.ShapeDtypeStruct((width // RING, tokens), BF16)] * RING,
        name="partial",
        cost_estimate=pl.CostEstimate(
            flops=2 * hid * tokens * width, bytes_accessed=9_000_000, transcendentals=0
        ),
    )(hidden_grad, ordered)
    arrived = [turn(parts[2], True, 2)]
    arrived += [turn(parts[1], True, 1), turn(parts[3], True, 3)]
    stage = add_up([parts[0]] + arrived).astype(BF16)
    depth = stage.shape[0] // RING
    stage = scatter_sum([stage[d * depth : (d + 1) * depth] for d in range(RING)], False).astype(BF16)
    depth = stage.shape[0] // RING
    shares = [lax.dynamic_slice_in_dim(stage, ((zl + d) % RING) * depth, depth, axis=0) for d in range(RING)]
    input_grad = add_up(shares[:1] + [shift(shares[d], "zl", d) for d in range(1, RING)]).astype(BF16)
    return (hidden.T, input_grad.T, up_grad)


def solution(mesh):
    inner = Mesh(mesh.devices.reshape(RING, RING, RING, RING, 2), ("y", "x", "zl", "zh", "c"))
    tokens, features = ("zh", "c"), ("y", "x", "zl")
    return jax.shard_map(
        work,
        mesh=inner,
        in_specs=(P(tokens, features), P(tokens, features), P(features, None)),
        out_specs=(P(tokens, features), P(tokens, features), P(features, None)),
        check_vma=False,
    )
```

```python
import jax
import jax.numpy as jnp
from jax import lax
from jax.experimental import pallas as pl
from jax.experimental.pallas import tpu as pltpu
from jax.sharding import Mesh
from jax.sharding import PartitionSpec as P


inv_sqrt_two = 0.7071067811865476
inv_sqrt_two_pi = 0.3989422804014327


RING = 4
F32 = jnp.float32
BF16 = jnp.bfloat16


def gelu_parts(preact):
    normal_cdf = 0.5 * (1.0 + lax.erf(preact * inv_sqrt_two))
    gelu_out = preact * normal_cdf
    gelu_slope = normal_cdf + preact * jnp.exp(-0.5 * preact * preact) * inv_sqrt_two_pi
    return (gelu_out, gelu_slope)


def shift(value, axis, by):
    size = lax.axis_size(axis)
    return lax.ppermute(value, axis, [(i, (i + by) % size) for i in range(size)])


def dot(left, right, dims):
    return lax.dot_general(left, right, (dims, ((), ())), preferred_element_type=F32)


def spot_of(pos_ref, outer, inner):
    core = pos_ref[2]
    dy = outer + core * (inner - outer)
    dx = inner + core * (outer - inner)
    return lax.rem(pos_ref[0] + dy, RING), lax.rem(pos_ref[1] + dx, RING)


def column_of(pos_ref, outer, inner, width):
    y, x = spot_of(pos_ref, outer, inner)
    return pl.multiple_of((y * RING + x) * width, 128)


def order_kernel(pos_ref, up_ref, out_ref):
    width = up_ref.shape[1] // (RING * RING)
    for outer in range(RING):
        for inner in range(RING):
            out_ref[:, pl.ds((outer * RING + inner) * width, width)] = up_ref[
                :, pl.ds(column_of(pos_ref, outer, inner, width), width)
            ]


def early_kernel(up_ref, *refs):
    total_ref = refs[-1]
    depth = refs[0].shape[0]
    total = None
    for place, ref in zip((0, 1, 2, 3, 6, 7), refs[:-1]):
        term = dot(up_ref[:, pl.ds(place * depth, depth)], ref[...], ((1,), (0,)))
        total = term if total is None else total + term
    total_ref[...] = total


def forward_kernel(pos_ref, *refs):
    pieces = refs[0 : 2 * RING]
    early_ref, cot_ref, up_ref, hidden_ref, grad_ref, keep_ref, send_ref, packed_ref, term_ref = refs[2 * RING :]
    depth = pieces[0].shape[0]
    width = depth // 2
    rows = keep_ref.shape[1]
    total = early_ref[...]
    for place in (4, 5):
        total += dot(up_ref[:, pl.ds(place * depth, depth)], pieces[place][...], ((1,), (0,)))
    gelu_out, gelu_slope = gelu_parts(total)
    hidden_ref[...] = gelu_out.astype(BF16)
    grad_ref[...] = (cot_ref[...].astype(F32) * gelu_slope).astype(BF16)
    core, zh = pos_ref[2], pos_ref[3]
    for at, half in enumerate((core, 1 - core)):
        packed_ref[pl.ds(at * rows, rows), :] = grad_ref[pl.ds(pl.multiple_of(half * rows, 16), rows), :]
    grads = packed_ref[...]
    for place, piece in enumerate(pieces):
        term = dot(grads, piece[...], ((1,), (1,))).astype(BF16)
        for part in range(2):
            block = 2 * place + part
            y, x = spot_of(pos_ref, block // RING, block % RING)
            quarter = lax.rem(y + RING - zh, RING)
            where = pl.ds(pl.multiple_of(x * width, 128), width)
            for at in range(2):
                term_ref[at, quarter, :, where] = term[at * rows : (at + 1) * rows, part * width : (part + 1) * width]
    near, away = 1 + 2 * core, 3 - 2 * core
    for at, (half, quarter) in enumerate(((0, 2), (1, near), (0, near), (0, 0), (1, 0))):
        keep_ref[at] = term_ref[half, quarter]
    for at, (half, quarter) in enumerate(((1, 2), (0, away), (1, away), (1, 0), (0, 0))):
        send_ref[at] = term_ref[half, quarter]


def input_grad_kernel(grad_ref, up_ref, *outs):
    grads = grad_ref[...]
    depth = outs[0].shape[0]
    for d in range(RING):
        term = dot(up_ref[:, pl.ds(d * depth, depth)], grads, ((0,), (0,)))
        outs[d][...] = term.astype(BF16)


def place_kernel(pos_ref, mine_ref, next_ref, far_ref, other_next_ref, other_far_ref, out_ref):
    core, zh = pos_ref[2], pos_ref[3]
    rows, depth = far_ref.shape
    lead = pl.ds(pl.multiple_of(core * rows, 16), rows)
    follow = pl.ds(pl.multiple_of((1 - core) * rows, 16), rows)

    def at(d):
        return pl.ds(pl.multiple_of(lax.rem(zh + d, RING) * depth, 128), depth)

    out_ref[lead, at(0)] = mine_ref[0]
    out_ref[follow, at(0)] = mine_ref[1]
    out_ref[lead, at(3 - 2 * core)] = next_ref[0]
    out_ref[follow, at(3 - 2 * core)] = next_ref[1]
    out_ref[follow, at(1 + 2 * core)] = other_next_ref[0]
    out_ref[lead, at(1 + 2 * core)] = other_next_ref[1]
    out_ref[lead, at(2)] = far_ref[...]
    out_ref[follow, at(2)] = other_far_ref[...]


def vmem(count):
    return [pl.BlockSpec(memory_space=pltpu.VMEM)] * count


def turn(value, late, by):
    def target(y, x, c):
        if (c == 0) != late:
            return (y, (x + by) % RING, c)
        return ((y + by) % RING, x, c)

    def flat(y, x, c):
        return (y * RING + x) * 2 + c

    spots = [(y, x, c) for y in range(RING) for x in range(RING) for c in range(2)]
    return lax.ppermute(value, ("y", "x", "c"), [(flat(*s), flat(*target(*s))) for s in spots])


def advance(value):
    pairs = []
    for zh in range(RING):
        pairs += [(zh * 2, (zh + 1) % RING * 2), (zh * 2 + 1, (zh - 1) % RING * 2 + 1)]
    return lax.ppermute(value, ("zh", "c"), pairs)


def gather(value, late):
    return [value] + [turn(value, late, -d) for d in range(1, RING)]


def add_up(values):
    total = values[0].astype(F32)
    for value in values[1:]:
        total = total + value.astype(F32)
    return total


def scatter_sum(values, late):
    return add_up([values[0]] + [turn(values[d], late, d) for d in range(1, RING)])


def work(normed, hidden_cot, up_rows):
    y, x, zl, zh, core = (lax.axis_index(a) for a in ("y", "x", "zl", "zh", "c"))
    pos = jnp.stack([y, x, core, zh]).astype(jnp.int32)
    hid, width = up_rows.shape
    tokens = normed.shape[0]
    scalars = pl.BlockSpec(memory_space=pltpu.SMEM)

    ordered = pl.pallas_call(
        order_kernel,
        in_specs=[scalars] + vmem(1),
        out_specs=vmem(1)[0],
        out_shape=jax.ShapeDtypeStruct((hid, width), BF16),
        name="order",
        cost_estimate=pl.CostEstimate(flops=0, bytes_accessed=4 * hid * width, transcendentals=0),
    )(pos, up_rows)

    block = lax.all_gather(normed.T, "zl", axis=0, tiled=True)
    quarters = gather(block, False)
    upper, lower = jnp.concatenate(quarters[:2], axis=0), jnp.concatenate(quarters[2:], axis=0)
    upper1, lower3 = turn(upper, True, -1), turn(lower, True, 1)
    lower1, upper3 = turn(lower, True, -1), turn(upper, True, 1)
    upper2, lower2 = turn(upper1, True, -1), turn(lower3, True, 1)
    pieces = [upper, lower, upper1, lower1, upper2, lower2, upper3, lower3]
    early = pl.pallas_call(
        early_kernel,
        in_specs=vmem(7),
        out_specs=vmem(1)[0],
        out_shape=jax.ShapeDtypeStruct((hid, tokens), F32),
        name="early",
        cost_estimate=pl.CostEstimate(flops=3 * hid * tokens * width // 2, bytes_accessed=7_000_000, transcendentals=0),
    )(ordered, *pieces[:4], *pieces[6:])

    hidden, hidden_grad, keep, send = pl.pallas_call(
        forward_kernel,
        in_specs=[scalars] + vmem(2 * RING + 3),
        out_specs=vmem(4),
        out_shape=[jax.ShapeDtypeStruct((hid, tokens), BF16)] * 2
        + [jax.ShapeDtypeStruct((5, hid // 2, width // RING), BF16)] * 2,
        scratch_shapes=[
            pltpu.VMEM((hid, tokens), BF16),
            pltpu.VMEM((2, RING, hid // 2, width // RING), BF16),
        ],
        name="forward",
        cost_estimate=pl.CostEstimate(
            flops=3 * hid * tokens * width, bytes_accessed=14_000_000, transcendentals=hid * tokens * 2
        ),
    )(pos, *pieces, early, hidden_cot.T, ordered)

    arrived = shift(send, "c", 1)
    opposite, follow, lead = (add_up([keep[at], arrived[at]]) for at in range(3))
    passed = advance(opposite.astype(BF16))
    follow_in = advance(follow.astype(BF16))
    lead_in = advance((lead + passed.astype(F32)).astype(BF16))
    other_in = shift(jnp.stack([follow_in, lead_in]), "c", 1)

    def finish(at, here, there):
        left, right = jnp.where(core == 0, here, there), jnp.where(core == 0, there, here)
        return (add_up([keep[at], arrived[at], left, right]) / (2 * RING)).astype(BF16)

    mine_lead, mine_follow = finish(3, lead_in, other_in[0]), finish(4, follow_in, other_in[1])
    next_lead = advance(mine_lead)
    next_follow = advance(mine_follow)
    far = advance(next_lead)
    near = jnp.stack([next_lead, next_follow])
    other_near = shift(near, "c", 1)
    other_far = shift(far, "c", 1)
    up_grad = pl.pallas_call(
        place_kernel,
        in_specs=[scalars] + vmem(5),
        out_specs=vmem(1)[0],
        out_shape=jax.ShapeDtypeStruct((hid, width), BF16),
        name="place",
        cost_estimate=pl.CostEstimate(flops=0, bytes_accessed=4 * hid * width, transcendentals=0),
    )(pos, jnp.stack([mine_lead, mine_follow]), near, far, other_near, other_far)

    parts = pl.pallas_call(
        input_grad_kernel,
        in_specs=vmem(2),
        out_specs=vmem(RING),
        out_shape=[jax.ShapeDtypeStruct((width // RING, tokens), BF16)] * RING,
        name="partial",
        cost_estimate=pl.CostEstimate(
            flops=2 * hid * tokens * width, bytes_accessed=9_000_000, transcendentals=0
        ),
    )(hidden_grad, ordered)
    stage = scatter_sum(parts, True).astype(BF16)
    depth = stage.shape[0] // RING
    stage = scatter_sum([stage[d * depth : (d + 1) * depth] for d in range(RING)], False).astype(BF16)
    depth = stage.shape[0] // RING
    shares = [lax.dynamic_slice_in_dim(stage, ((zl + d) % RING) * depth, depth, axis=0) for d in range(RING)]
    input_grad = add_up(shares[:1] + [shift(shares[d], "zl", d) for d in range(1, RING)]).astype(BF16)
    return (hidden.T, input_grad.T, up_grad)


def solution(mesh):
    inner = Mesh(mesh.devices.reshape(RING, RING, RING, RING, 2), ("y", "x", "zl", "zh", "c"))
    tokens, features = ("zh", "c"), ("y", "x", "zl")
    return jax.shard_map(
        work,
        mesh=inner,
        in_specs=(P(tokens, features), P(tokens, features), P(features, None)),
        out_specs=(P(tokens, features), P(tokens, features), P(features, None)),
        check_vma=False,
    )
```

```python
import jax
import jax.numpy as jnp
from jax import lax
from jax.experimental import pallas as pl
from jax.experimental.pallas import tpu as pltpu
from jax.sharding import Mesh
from jax.sharding import PartitionSpec as P


inv_sqrt_two = 0.7071067811865476
inv_sqrt_two_pi = 0.3989422804014327


RING = 4
F32 = jnp.float32
BF16 = jnp.bfloat16


def gelu_parts(preact):
    normal_cdf = 0.5 * (1.0 + lax.erf(preact * inv_sqrt_two))
    gelu_out = preact * normal_cdf
    gelu_slope = normal_cdf + preact * jnp.exp(-0.5 * preact * preact) * inv_sqrt_two_pi
    return (gelu_out, gelu_slope)


def shift(value, axis, by):
    size = lax.axis_size(axis)
    return lax.ppermute(value, axis, [(i, (i + by) % size) for i in range(size)])


def dot(left, right, dims):
    return lax.dot_general(left, right, (dims, ((), ())), preferred_element_type=F32)


def spot_of(pos_ref, outer, inner):
    core = pos_ref[2]
    dy = outer + core * (inner - outer)
    dx = inner + core * (outer - inner)
    return lax.rem(pos_ref[0] + dy, RING), lax.rem(pos_ref[1] + dx, RING)


def column_of(pos_ref, outer, inner, width):
    y, x = spot_of(pos_ref, outer, inner)
    return pl.multiple_of((y * RING + x) * width, 128)


def order_kernel(pos_ref, up_ref, out_ref):
    width = up_ref.shape[1] // (RING * RING)
    for outer in range(RING):
        for inner in range(RING):
            out_ref[:, pl.ds((outer * RING + inner) * width, width)] = up_ref[
                :, pl.ds(column_of(pos_ref, outer, inner, width), width)
            ]


def early_kernel(up_ref, *refs):
    total_ref = refs[-1]
    depth = refs[0].shape[0]
    total = None
    for place, ref in zip((0, 1, 2, 3, 6, 7), refs[:-1]):
        term = dot(up_ref[:, pl.ds(place * depth, depth)], ref[...], ((1,), (0,)))
        total = term if total is None else total + term
    total_ref[...] = total


def forward_kernel(pos_ref, *refs):
    pieces = refs[0 : 2 * RING]
    early_ref, cot_ref, up_ref, hidden_ref, grad_ref, keep_ref, send_ref, packed_ref, term_ref = refs[2 * RING :]
    depth = pieces[0].shape[0]
    width = depth // 2
    rows = keep_ref.shape[1]
    total = early_ref[...]
    for place in (4, 5):
        total += dot(up_ref[:, pl.ds(place * depth, depth)], pieces[place][...], ((1,), (0,)))
    gelu_out, gelu_slope = gelu_parts(total)
    hidden_ref[...] = gelu_out.astype(BF16)
    grad_ref[...] = (cot_ref[...].astype(F32) * gelu_slope).astype(BF16)
    core, zh = pos_ref[2], pos_ref[3]
    for at, half in enumerate((core, 1 - core)):
        packed_ref[pl.ds(at * rows, rows), :] = grad_ref[pl.ds(pl.multiple_of(half * rows, 16), rows), :]
    grads = packed_ref[...]
    for place, piece in enumerate(pieces):
        term = dot(grads, piece[...], ((1,), (1,))).astype(BF16)
        for part in range(2):
            block = 2 * place + part
            y, x = spot_of(pos_ref, block // RING, block % RING)
            quarter = lax.rem(y + RING - zh, RING)
            where = pl.ds(pl.multiple_of(x * width, 128), width)
            for at in range(2):
                term_ref[at, quarter, :, where] = term[at * rows : (at + 1) * rows, part * width : (part + 1) * width]
    near, away = 1 + 2 * core, 3 - 2 * core
    for at, (half, quarter) in enumerate(((0, 2), (1, near), (0, near), (0, 0))):
        keep_ref[at] = term_ref[half, quarter]
    for at, (half, quarter) in enumerate(((1, 2), (0, away), (1, away), (1, 0))):
        send_ref[at] = term_ref[half, quarter]


def input_grad_kernel(grad_ref, up_ref, *outs):
    grads = grad_ref[...]
    depth = outs[0].shape[0]
    for d in range(RING):
        term = dot(up_ref[:, pl.ds(d * depth, depth)], grads, ((0,), (0,)))
        outs[d][...] = term.astype(BF16)


def place_kernel(pos_ref, *refs):
    core, zh = pos_ref[2], pos_ref[3]
    out_ref = refs[-1]
    rows, depth = refs[0].shape
    lead = pl.ds(pl.multiple_of(core * rows, 16), rows)
    follow = pl.ds(pl.multiple_of((1 - core) * rows, 16), rows)
    behind, ahead = 3 - 2 * core, 1 + 2 * core
    spots = ((lead, 0), (follow, 0), (lead, behind), (follow, behind), (follow, ahead), (lead, ahead), (lead, 2), (follow, 2))
    for ref, (where, d) in zip(refs[:-1], spots):
        out_ref[where, pl.ds(pl.multiple_of(lax.rem(zh + d, RING) * depth, 128), depth)] = ref[...]


def vmem(count):
    return [pl.BlockSpec(memory_space=pltpu.VMEM)] * count


def turn(value, late, by):
    def target(y, x, c):
        if (c == 0) != late:
            return (y, (x + by) % RING, c)
        return ((y + by) % RING, x, c)

    def flat(y, x, c):
        return (y * RING + x) * 2 + c

    spots = [(y, x, c) for y in range(RING) for x in range(RING) for c in range(2)]
    return lax.ppermute(value, ("y", "x", "c"), [(flat(*s), flat(*target(*s))) for s in spots])


def advance(value, cross=False):
    pairs = []
    for zh in range(RING):
        pairs += [
            (zh * 2, (zh + 1) % RING * 2 + cross),
            (zh * 2 + 1, (zh - 1) % RING * 2 + 1 - cross),
        ]
    return lax.ppermute(value, ("zh", "c"), pairs)


def gather(value, late):
    return [value] + [turn(value, late, -d) for d in range(1, RING)]


def add_up(values):
    total = values[0].astype(F32)
    for value in values[1:]:
        total = total + value.astype(F32)
    return total


def scatter_sum(values, late):
    return add_up([values[0]] + [turn(values[d], late, d) for d in range(1, RING)])


def work(normed, hidden_cot, up_rows):
    y, x, zl, zh, core = (lax.axis_index(a) for a in ("y", "x", "zl", "zh", "c"))
    pos = jnp.stack([y, x, core, zh]).astype(jnp.int32)
    hid, width = up_rows.shape
    tokens = normed.shape[0]
    scalars = pl.BlockSpec(memory_space=pltpu.SMEM)

    ordered = pl.pallas_call(
        order_kernel,
        in_specs=[scalars] + vmem(1),
        out_specs=vmem(1)[0],
        out_shape=jax.ShapeDtypeStruct((hid, width), BF16),
        name="order",
        cost_estimate=pl.CostEstimate(flops=0, bytes_accessed=4 * hid * width, transcendentals=0),
    )(pos, up_rows)

    share = normed.T
    shares = [share] + [shift(share, "zl", -d) for d in range(1, RING)]
    block = jnp.zeros((RING * share.shape[0], tokens), BF16)
    for d in range(RING):
        block = lax.dynamic_update_slice_in_dim(block, shares[d], (zl + d) % RING * share.shape[0], axis=0)
    quarters = gather(block, False)
    upper, lower = jnp.concatenate(quarters[:2], axis=0), jnp.concatenate(quarters[2:], axis=0)
    upper1, lower3 = turn(upper, True, -1), turn(lower, True, 1)
    lower1, upper3 = turn(lower, True, -1), turn(upper, True, 1)
    upper2, lower2 = turn(upper1, True, -1), turn(lower3, True, 1)
    pieces = [upper, lower, upper1, lower1, upper2, lower2, upper3, lower3]
    early = pl.pallas_call(
        early_kernel,
        in_specs=vmem(7),
        out_specs=vmem(1)[0],
        out_shape=jax.ShapeDtypeStruct((hid, tokens), F32),
        name="early",
        cost_estimate=pl.CostEstimate(flops=3 * hid * tokens * width // 2, bytes_accessed=7_000_000, transcendentals=0),
    )(ordered, *pieces[:4], *pieces[6:])

    hidden, hidden_grad, keep, send = pl.pallas_call(
        forward_kernel,
        in_specs=[scalars] + vmem(2 * RING + 3),
        out_specs=vmem(4),
        out_shape=[jax.ShapeDtypeStruct((hid, tokens), BF16)] * 2
        + [jax.ShapeDtypeStruct((4, hid // 2, width // RING), BF16)] * 2,
        scratch_shapes=[
            pltpu.VMEM((hid, tokens), BF16),
            pltpu.VMEM((2, RING, hid // 2, width // RING), BF16),
        ],
        name="forward",
        cost_estimate=pl.CostEstimate(
            flops=3 * hid * tokens * width, bytes_accessed=14_000_000, transcendentals=hid * tokens * 2
        ),
    )(pos, *pieces, early, hidden_cot.T, ordered)

    arrived = shift(send, "c", 1)
    opposite, follow, lead = (add_up([keep[at], arrived[at]]) for at in range(3))
    passed = advance(opposite.astype(BF16))
    cross_in = advance(follow.astype(BF16), cross=True)
    lead_in = advance((lead + passed.astype(F32)).astype(BF16))
    mine = (add_up([keep[3], arrived[3], cross_in, lead_in]) / (2 * RING)).astype(BF16)
    next_lead = advance(mine)
    other_mine = shift(mine, "c", 1)
    next_follow = advance(other_mine)
    far = advance(next_lead)
    other_next_lead = shift(next_lead, "c", 1)
    other_next_follow = shift(next_follow, "c", 1)
    other_far = shift(far, "c", 1)
    up_grad = pl.pallas_call(
        place_kernel,
        in_specs=[scalars] + vmem(8),
        out_specs=vmem(1)[0],
        out_shape=jax.ShapeDtypeStruct((hid, width), BF16),
        name="place",
        cost_estimate=pl.CostEstimate(flops=0, bytes_accessed=4 * hid * width, transcendentals=0),
    )(pos, mine, other_mine, next_lead, next_follow, other_next_lead, other_next_follow, far, other_far)

    parts = pl.pallas_call(
        input_grad_kernel,
        in_specs=vmem(2),
        out_specs=vmem(RING),
        out_shape=[jax.ShapeDtypeStruct((width // RING, tokens), BF16)] * RING,
        name="partial",
        cost_estimate=pl.CostEstimate(
            flops=2 * hid * tokens * width, bytes_accessed=9_000_000, transcendentals=0
        ),
    )(hidden_grad, ordered)
    stage = scatter_sum(parts, True).astype(BF16)
    depth = stage.shape[0] // RING
    stage = scatter_sum([stage[d * depth : (d + 1) * depth] for d in range(RING)], False).astype(BF16)
    depth = stage.shape[0] // RING
    shares = [lax.dynamic_slice_in_dim(stage, ((zl + d) % RING) * depth, depth, axis=0) for d in range(RING)]
    input_grad = add_up(shares[:1] + [shift(shares[d], "zl", d) for d in range(1, RING)]).astype(BF16)
    return (hidden.T, input_grad.T, up_grad)


def solution(mesh):
    inner = Mesh(mesh.devices.reshape(RING, RING, RING, RING, 2), ("y", "x", "zl", "zh", "c"))
    tokens, features = ("zh", "c"), ("y", "x", "zl")
    return jax.shard_map(
        work,
        mesh=inner,
        in_specs=(P(tokens, features), P(tokens, features), P(features, None)),
        out_specs=(P(tokens, features), P(tokens, features), P(features, None)),
        check_vma=False,
    )
```

```python
import jax
import jax.numpy as jnp
from jax import lax
from jax.experimental import pallas as pl
from jax.experimental.pallas import tpu as pltpu
from jax.sharding import Mesh
from jax.sharding import PartitionSpec as P


inv_sqrt_two = 0.7071067811865476
inv_sqrt_two_pi = 0.3989422804014327


RING = 4
F32 = jnp.float32
BF16 = jnp.bfloat16


def gelu_parts(preact):
    normal_cdf = 0.5 * (1.0 + lax.erf(preact * inv_sqrt_two))
    gelu_out = preact * normal_cdf
    gelu_slope = normal_cdf + preact * jnp.exp(-0.5 * preact * preact) * inv_sqrt_two_pi
    return (gelu_out, gelu_slope)


def shift(value, axis, by):
    size = lax.axis_size(axis)
    return lax.ppermute(value, axis, [(i, (i + by) % size) for i in range(size)])


def dot(left, right, dims):
    return lax.dot_general(left, right, (dims, ((), ())), preferred_element_type=F32)


def spot_of(pos_ref, outer, inner):
    core = pos_ref[2]
    dy = outer + core * (inner - outer)
    dx = inner + core * (outer - inner)
    return lax.rem(pos_ref[0] + dy, RING), lax.rem(pos_ref[1] + dx, RING)


def column_of(pos_ref, outer, inner, width):
    y, x = spot_of(pos_ref, outer, inner)
    return pl.multiple_of((y * RING + x) * width, 128)


def order_kernel(pos_ref, up_ref, out_ref):
    width = up_ref.shape[1] // (RING * RING)
    for outer in range(RING):
        for inner in range(RING):
            out_ref[:, pl.ds((outer * RING + inner) * width, width)] = up_ref[
                :, pl.ds(column_of(pos_ref, outer, inner, width), width)
            ]


def early_kernel(up_ref, *refs):
    total_ref = refs[-1]
    depth = refs[0].shape[0]
    total = None
    for place, ref in zip((0, 1, 2, 3, 6, 7), refs[:-1]):
        term = dot(up_ref[:, pl.ds(place * depth, depth)], ref[...], ((1,), (0,)))
        total = term if total is None else total + term
    total_ref[...] = total


def forward_kernel(pos_ref, *refs):
    pieces = refs[0 : 2 * RING]
    early_ref, cot_ref, up_ref, hidden_ref, grad_ref, keep_ref, send_ref, packed_ref, term_ref = refs[2 * RING :]
    depth = pieces[0].shape[0]
    width = depth // 2
    rows = keep_ref.shape[1]
    total = early_ref[...]
    for place in (4, 5):
        total += dot(up_ref[:, pl.ds(place * depth, depth)], pieces[place][...], ((1,), (0,)))
    gelu_out, gelu_slope = gelu_parts(total)
    hidden_ref[...] = gelu_out.astype(BF16)
    grad_ref[...] = (cot_ref[...].astype(F32) * gelu_slope).astype(BF16)
    core, zh = pos_ref[2], pos_ref[3]
    for at, half in enumerate((core, 1 - core)):
        packed_ref[pl.ds(at * rows, rows), :] = grad_ref[pl.ds(pl.multiple_of(half * rows, 16), rows), :]
    grads = packed_ref[...]
    for place, piece in enumerate(pieces):
        term = dot(grads, piece[...], ((1,), (1,))).astype(BF16)
        for part in range(2):
            block = 2 * place + part
            y, x = spot_of(pos_ref, block // RING, block % RING)
            quarter = lax.rem(y + RING - zh, RING)
            where = pl.ds(pl.multiple_of(x * width, 128), width)
            for at in range(2):
                term_ref[at, quarter, :, where] = term[at * rows : (at + 1) * rows, part * width : (part + 1) * width]
    near, away = 1 + 2 * core, 3 - 2 * core
    for at, (half, quarter) in enumerate(((0, 2), (1, near), (0, near), (0, 0))):
        keep_ref[at] = term_ref[half, quarter]
    for at, (half, quarter) in enumerate(((1, 2), (0, away), (1, away), (1, 0))):
        send_ref[at] = term_ref[half, quarter]


def input_grad_kernel(grad_ref, up_ref, *outs):
    grads = grad_ref[...]
    depth = outs[0].shape[0]
    for d in range(RING):
        term = dot(up_ref[:, pl.ds(d * depth, depth)], grads, ((0,), (0,)))
        outs[d][...] = term.astype(BF16)


def place_kernel(pos_ref, *refs):
    core, zh = pos_ref[2], pos_ref[3]
    pieces, (out_ref, whole_ref, sems) = refs[:8], refs[8:]
    rows, depth = pieces[0].shape
    behind, ahead = 3 - 2 * core, 1 + 2 * core
    halves = []
    for half, places in ((core, ((0, 0), (2, behind), (5, ahead), (6, 2))), (1 - core, ((1, 0), (3, behind), (4, ahead), (7, 2)))):
        where = pl.ds(pl.multiple_of(half * rows, 16), rows)
        copies = []
        for at, d in places:
            columns = pl.ds(pl.multiple_of(lax.rem(zh + d, RING) * depth, 128), depth)
            copies.append(pltpu.make_async_copy(pieces[at], whole_ref.at[where, columns], sems.at[at]))
            copies[-1].start()
        halves.append((where, copies))
    outs = []
    for at, (where, copies) in enumerate(halves):
        for copy in copies:
            copy.wait()
        outs.append(pltpu.make_async_copy(whole_ref.at[where, :], out_ref.at[where, :], sems.at[8 + at]))
        outs[-1].start()
    for copy in outs:
        copy.wait()


def vmem(count):
    return [pl.BlockSpec(memory_space=pltpu.VMEM)] * count


def turn(value, late, by):
    def target(y, x, c):
        if (c == 0) != late:
            return (y, (x + by) % RING, c)
        return ((y + by) % RING, x, c)

    def flat(y, x, c):
        return (y * RING + x) * 2 + c

    spots = [(y, x, c) for y in range(RING) for x in range(RING) for c in range(2)]
    return lax.ppermute(value, ("y", "x", "c"), [(flat(*s), flat(*target(*s))) for s in spots])


def advance(value, cross=False):
    pairs = []
    for zh in range(RING):
        pairs += [
            (zh * 2, (zh + 1) % RING * 2 + cross),
            (zh * 2 + 1, (zh - 1) % RING * 2 + 1 - cross),
        ]
    return lax.ppermute(value, ("zh", "c"), pairs)


def gather(value, late):
    return [value] + [turn(value, late, -d) for d in range(1, RING)]


def add_up(values):
    total = values[0].astype(F32)
    for value in values[1:]:
        total = total + value.astype(F32)
    return total


def scatter_sum(values, late):
    return add_up([values[0]] + [turn(values[d], late, d) for d in range(1, RING)])


def work(normed, hidden_cot, up_rows):
    y, x, zl, zh, core = (lax.axis_index(a) for a in ("y", "x", "zl", "zh", "c"))
    pos = jnp.stack([y, x, core, zh]).astype(jnp.int32)
    hid, width = up_rows.shape
    tokens = normed.shape[0]
    scalars = pl.BlockSpec(memory_space=pltpu.SMEM)

    ordered = pl.pallas_call(
        order_kernel,
        in_specs=[scalars] + vmem(1),
        out_specs=vmem(1)[0],
        out_shape=jax.ShapeDtypeStruct((hid, width), BF16),
        name="order",
        cost_estimate=pl.CostEstimate(flops=0, bytes_accessed=4 * hid * width, transcendentals=0),
    )(pos, up_rows)

    share = normed.T
    shares = [share] + [shift(share, "zl", -d) for d in range(1, RING)]
    block = jnp.zeros((RING * share.shape[0], tokens), BF16)
    for d in range(RING):
        block = lax.dynamic_update_slice_in_dim(block, shares[d], (zl + d) % RING * share.shape[0], axis=0)
    quarters = gather(block, False)
    upper, lower = jnp.concatenate(quarters[:2], axis=0), jnp.concatenate(quarters[2:], axis=0)
    upper1, lower3 = turn(upper, True, -1), turn(lower, True, 1)
    lower1, upper3 = turn(lower, True, -1), turn(upper, True, 1)
    upper2, lower2 = turn(upper1, True, -1), turn(lower3, True, 1)
    pieces = [upper, lower, upper1, lower1, upper2, lower2, upper3, lower3]
    early = pl.pallas_call(
        early_kernel,
        in_specs=vmem(7),
        out_specs=vmem(1)[0],
        out_shape=jax.ShapeDtypeStruct((hid, tokens), F32),
        name="early",
        cost_estimate=pl.CostEstimate(flops=3 * hid * tokens * width // 2, bytes_accessed=7_000_000, transcendentals=0),
    )(ordered, *pieces[:4], *pieces[6:])

    hidden, hidden_grad, keep, send = pl.pallas_call(
        forward_kernel,
        in_specs=[scalars] + vmem(2 * RING + 3),
        out_specs=vmem(4),
        out_shape=[jax.ShapeDtypeStruct((hid, tokens), BF16)] * 2
        + [jax.ShapeDtypeStruct((4, hid // 2, width // RING), BF16)] * 2,
        scratch_shapes=[
            pltpu.VMEM((hid, tokens), BF16),
            pltpu.VMEM((2, RING, hid // 2, width // RING), BF16),
        ],
        name="forward",
        cost_estimate=pl.CostEstimate(
            flops=3 * hid * tokens * width, bytes_accessed=14_000_000, transcendentals=hid * tokens * 2
        ),
    )(pos, *pieces, early, hidden_cot.T, ordered)

    arrived = shift(send, "c", 1)
    opposite, follow, lead = (add_up([keep[at], arrived[at]]) for at in range(3))
    passed = advance(opposite.astype(BF16))
    cross_in = advance(follow.astype(BF16), cross=True)
    lead_in = advance((lead + passed.astype(F32)).astype(BF16))
    mine = (add_up([keep[3], arrived[3], cross_in, lead_in]) / (2 * RING)).astype(BF16)
    next_lead = advance(mine)
    other_mine = shift(mine, "c", 1)
    next_follow = advance(other_mine)
    far = advance(next_lead)
    other_next_lead = shift(next_lead, "c", 1)
    other_next_follow = shift(next_follow, "c", 1)
    other_far = shift(far, "c", 1)
    up_grad = pl.pallas_call(
        place_kernel,
        in_specs=[scalars] + [pl.BlockSpec(memory_space=pl.ANY)] * 8,
        out_specs=pl.BlockSpec(memory_space=pl.ANY),
        out_shape=jax.ShapeDtypeStruct((hid, width), BF16),
        scratch_shapes=[pltpu.VMEM((hid, width), BF16), pltpu.SemaphoreType.DMA((10,))],
        compiler_params=pltpu.CompilerParams(vmem_limit_bytes=8 << 20),
        name="place",
        cost_estimate=pl.CostEstimate(flops=0, bytes_accessed=4 * hid * width, transcendentals=0),
    )(pos, mine, other_mine, next_lead, next_follow, other_next_lead, other_next_follow, far, other_far)

    parts = pl.pallas_call(
        input_grad_kernel,
        in_specs=vmem(2),
        out_specs=vmem(RING),
        out_shape=[jax.ShapeDtypeStruct((width // RING, tokens), BF16)] * RING,
        name="partial",
        cost_estimate=pl.CostEstimate(
            flops=2 * hid * tokens * width, bytes_accessed=9_000_000, transcendentals=0
        ),
    )(hidden_grad, ordered)
    stage = scatter_sum(parts, True).astype(BF16)
    depth = stage.shape[0] // RING
    blocks = [stage[d * depth : (d + 1) * depth] for d in range(RING)]
    arrived = [turn(blocks[2], False, 2), turn(blocks[1], False, 1)]
    arrived += [turn(blocks[3], False, 3)]
    stage = add_up([blocks[0]] + arrived).astype(BF16)
    for bit in (2, 1):
        depth = stage.shape[0] // 2
        side = zl // bit % 2
        other = lax.dynamic_slice_in_dim(stage, (1 - side) * depth, depth, axis=0)
        arrived = lax.ppermute(other, "zl", [(i, i ^ bit) for i in range(RING)])
        stage = add_up([lax.dynamic_slice_in_dim(stage, side * depth, depth, axis=0), arrived]).astype(BF16)
    input_grad = stage
    return (hidden.T, input_grad.T, up_grad)


def solution(mesh):
    inner = Mesh(mesh.devices.reshape(RING, RING, RING, RING, 2), ("y", "x", "zl", "zh", "c"))
    tokens, features = ("zh", "c"), ("y", "x", "zl")
    return jax.shard_map(
        work,
        mesh=inner,
        in_specs=(P(tokens, features), P(tokens, features), P(features, None)),
        out_specs=(P(tokens, features), P(tokens, features), P(features, None)),
        check_vma=False,
    )
```

```python
import jax
import jax.numpy as jnp
from jax import lax
from jax.experimental import pallas as pl
from jax.experimental.pallas import tpu as pltpu
from jax.sharding import Mesh
from jax.sharding import PartitionSpec as P


inv_sqrt_two = 0.7071067811865476
inv_sqrt_two_pi = 0.3989422804014327


RING = 4
F32 = jnp.float32
BF16 = jnp.bfloat16


def gelu_parts(preact):
    normal_cdf = 0.5 * (1.0 + lax.erf(preact * inv_sqrt_two))
    gelu_out = preact * normal_cdf
    gelu_slope = normal_cdf + preact * jnp.exp(-0.5 * preact * preact) * inv_sqrt_two_pi
    return (gelu_out, gelu_slope)


def shift(value, axis, by):
    size = lax.axis_size(axis)
    return lax.ppermute(value, axis, [(i, (i + by) % size) for i in range(size)])


def dot(left, right, dims):
    return lax.dot_general(left, right, (dims, ((), ())), preferred_element_type=F32)


def spot_of(pos_ref, outer, inner):
    core = pos_ref[2]
    dy = outer + core * (inner - outer)
    dx = inner + core * (outer - inner)
    return lax.rem(pos_ref[0] + dy, RING), lax.rem(pos_ref[1] + dx, RING)


def column_of(pos_ref, outer, inner, width):
    y, x = spot_of(pos_ref, outer, inner)
    return pl.multiple_of((y * RING + x) * width, 128)


def order_kernel(pos_ref, up_ref, out_ref):
    width = up_ref.shape[1] // (RING * RING)
    for outer in range(RING):
        for inner in range(RING):
            out_ref[:, pl.ds((outer * RING + inner) * width, width)] = up_ref[
                :, pl.ds(column_of(pos_ref, outer, inner, width), width)
            ]


def early_kernel(up_ref, *refs):
    total_ref = refs[-1]
    depth = refs[0].shape[0]
    total = None
    for place, ref in zip((0, 1, 2, 3, 6, 7), refs[:-1]):
        term = dot(up_ref[:, pl.ds(place * depth, depth)], ref[...], ((1,), (0,)))
        total = term if total is None else total + term
    total_ref[...] = total


def forward_kernel(pos_ref, *refs):
    pieces = refs[0 : 2 * RING]
    early_ref, cot_ref, up_ref, hidden_ref, grad_ref, keep_ref, send_ref, packed_ref, term_ref = refs[2 * RING :]
    depth = pieces[0].shape[0]
    width = depth // 2
    rows = keep_ref.shape[1]
    total = early_ref[...]
    for place in (4, 5):
        total += dot(up_ref[:, pl.ds(place * depth, depth)], pieces[place][...], ((1,), (0,)))
    gelu_out, gelu_slope = gelu_parts(total)
    hidden_ref[...] = gelu_out.astype(BF16)
    grad_ref[...] = (cot_ref[...].astype(F32) * gelu_slope).astype(BF16)
    core, zh = pos_ref[2], pos_ref[3]
    for at, half in enumerate((core, 1 - core)):
        packed_ref[pl.ds(at * rows, rows), :] = grad_ref[pl.ds(pl.multiple_of(half * rows, 16), rows), :]
    grads = packed_ref[...]
    for place, piece in enumerate(pieces):
        term = dot(grads, piece[...], ((1,), (1,))).astype(BF16)
        for part in range(2):
            block = 2 * place + part
            y, x = spot_of(pos_ref, block // RING, block % RING)
            quarter = lax.rem(y + RING - zh, RING)
            where = pl.ds(pl.multiple_of(x * width, 128), width)
            for at in range(2):
                term_ref[at, quarter, :, where] = term[at * rows : (at + 1) * rows, part * width : (part + 1) * width]
    near, away = 1 + 2 * core, 3 - 2 * core
    for at, (half, quarter) in enumerate(((0, 2), (1, near), (0, near), (0, 0))):
        keep_ref[at] = term_ref[half, quarter]
    for at, (half, quarter) in enumerate(((1, 2), (0, away), (1, away), (1, 0))):
        send_ref[at] = term_ref[half, quarter]


def input_grad_kernel(grad_ref, up_ref, *outs):
    grads = grad_ref[...]
    depth = outs[0].shape[0]
    for d in range(RING):
        term = dot(up_ref[:, pl.ds(d * depth, depth)], grads, ((0,), (0,)))
        outs[d][...] = term.astype(BF16)


def place_kernel(pos_ref, *refs):
    core, zh = pos_ref[2], pos_ref[3]
    pieces, (out_ref, whole_ref, sems) = refs[:8], refs[8:]
    rows, depth = pieces[0].shape
    behind, ahead = 3 - 2 * core, 1 + 2 * core
    halves = []
    for half, places in ((core, ((0, 0), (2, behind), (5, ahead), (6, 2))), (1 - core, ((1, 0), (3, behind), (4, ahead), (7, 2)))):
        where = pl.ds(pl.multiple_of(half * rows, 16), rows)
        copies = []
        for at, d in places:
            columns = pl.ds(pl.multiple_of(lax.rem(zh + d, RING) * depth, 128), depth)
            copies.append(pltpu.make_async_copy(pieces[at], whole_ref.at[where, columns], sems.at[at]))
            copies[-1].start()
        halves.append((where, copies))
    outs = []
    for at, (where, copies) in enumerate(halves):
        for copy in copies:
            copy.wait()
        outs.append(pltpu.make_async_copy(whole_ref.at[where, :], out_ref.at[where, :], sems.at[8 + at]))
        outs[-1].start()
    for copy in outs:
        copy.wait()


def vmem(count):
    return [pl.BlockSpec(memory_space=pltpu.VMEM)] * count


def turn(value, late, by):
    def target(y, x, c):
        if (c == 0) != late:
            return (y, (x + by) % RING, c)
        return ((y + by) % RING, x, c)

    def flat(y, x, c):
        return (y * RING + x) * 2 + c

    spots = [(y, x, c) for y in range(RING) for x in range(RING) for c in range(2)]
    return lax.ppermute(value, ("y", "x", "c"), [(flat(*s), flat(*target(*s))) for s in spots])


def advance(value, cross=False):
    pairs = []
    for zh in range(RING):
        pairs += [
            (zh * 2, (zh + 1) % RING * 2 + cross),
            (zh * 2 + 1, (zh - 1) % RING * 2 + 1 - cross),
        ]
    return lax.ppermute(value, ("zh", "c"), pairs)


def gather(value, late):
    return [value] + [turn(value, late, -d) for d in range(1, RING)]


def add_up(values):
    total = values[0].astype(F32)
    for value in values[1:]:
        total = total + value.astype(F32)
    return total


def scatter_sum(values, late):
    return add_up([values[0]] + [turn(values[d], late, d) for d in range(1, RING)])


def work(normed, hidden_cot, up_rows):
    y, x, zl, zh, core = (lax.axis_index(a) for a in ("y", "x", "zl", "zh", "c"))
    pos = jnp.stack([y, x, core, zh]).astype(jnp.int32)
    hid, width = up_rows.shape
    tokens = normed.shape[0]
    scalars = pl.BlockSpec(memory_space=pltpu.SMEM)

    ordered = pl.pallas_call(
        order_kernel,
        in_specs=[scalars] + vmem(1),
        out_specs=vmem(1)[0],
        out_shape=jax.ShapeDtypeStruct((hid, width), BF16),
        name="order",
        cost_estimate=pl.CostEstimate(flops=0, bytes_accessed=4 * hid * width, transcendentals=0),
    )(pos, up_rows)

    share = normed.T
    shares = [share] + [shift(share, "zl", -d) for d in range(1, RING)]
    block = jnp.zeros((RING * share.shape[0], tokens), BF16)
    for d in range(RING):
        block = lax.dynamic_update_slice_in_dim(block, shares[d], (zl + d) % RING * share.shape[0], axis=0)
    quarters = gather(block, False)
    upper, lower = jnp.concatenate(quarters[:2], axis=0), jnp.concatenate(quarters[2:], axis=0)
    upper1, lower3 = turn(upper, True, -1), turn(lower, True, 1)
    lower1, upper3 = turn(lower, True, -1), turn(upper, True, 1)
    upper2, lower2 = turn(upper1, True, -1), turn(lower3, True, 1)
    pieces = [upper, lower, upper1, lower1, upper2, lower2, upper3, lower3]
    early = pl.pallas_call(
        early_kernel,
        in_specs=vmem(7),
        out_specs=vmem(1)[0],
        out_shape=jax.ShapeDtypeStruct((hid, tokens), F32),
        name="early",
        cost_estimate=pl.CostEstimate(flops=3 * hid * tokens * width // 2, bytes_accessed=7_000_000, transcendentals=0),
    )(ordered, *pieces[:4], *pieces[6:])

    hidden, hidden_grad, keep, send = pl.pallas_call(
        forward_kernel,
        in_specs=[scalars] + vmem(2 * RING + 3),
        out_specs=vmem(4),
        out_shape=[jax.ShapeDtypeStruct((hid, tokens), BF16)] * 2
        + [jax.ShapeDtypeStruct((4, hid // 2, width // RING), BF16)] * 2,
        scratch_shapes=[
            pltpu.VMEM((hid, tokens), BF16),
            pltpu.VMEM((2, RING, hid // 2, width // RING), BF16),
        ],
        name="forward",
        cost_estimate=pl.CostEstimate(
            flops=3 * hid * tokens * width, bytes_accessed=14_000_000, transcendentals=hid * tokens * 2
        ),
    )(pos, *pieces, early, hidden_cot.T, ordered)

    arrived = shift(send, "c", 1)
    opposite, follow, lead = (add_up([keep[at], arrived[at]]) for at in range(3))
    passed = advance(opposite.astype(BF16))
    cross_in = advance(follow.astype(BF16), cross=True)
    lead_in = advance((lead + passed.astype(F32)).astype(BF16))
    mine = (add_up([keep[3], arrived[3], cross_in, lead_in]) / (2 * RING)).astype(BF16)
    next_lead = advance(mine)
    other_mine = shift(mine, "c", 1)
    next_follow = advance(other_mine)
    far = advance(next_lead)
    other_next_lead = shift(next_lead, "c", 1)
    other_next_follow = shift(next_follow, "c", 1)
    other_far = shift(far, "c", 1)
    up_grad = pl.pallas_call(
        place_kernel,
        in_specs=[scalars] + [pl.BlockSpec(memory_space=pl.ANY)] * 8,
        out_specs=pl.BlockSpec(memory_space=pl.ANY),
        out_shape=jax.ShapeDtypeStruct((hid, width), BF16),
        scratch_shapes=[pltpu.VMEM((hid, width), BF16), pltpu.SemaphoreType.DMA((10,))],
        compiler_params=pltpu.CompilerParams(vmem_limit_bytes=8 << 20),
        name="place",
        cost_estimate=pl.CostEstimate(flops=0, bytes_accessed=4 * hid * width, transcendentals=0),
    )(pos, mine, other_mine, next_lead, next_follow, other_next_lead, other_next_follow, far, other_far)

    parts = pl.pallas_call(
        input_grad_kernel,
        in_specs=vmem(2),
        out_specs=vmem(RING),
        out_shape=[jax.ShapeDtypeStruct((width // RING, tokens), BF16)] * RING,
        name="partial",
        cost_estimate=pl.CostEstimate(
            flops=2 * hid * tokens * width, bytes_accessed=9_000_000, transcendentals=0
        ),
    )(hidden_grad, ordered)
    stage = scatter_sum(parts, True).astype(BF16)
    depth = stage.shape[0] // RING
    blocks = [stage[d * depth : (d + 1) * depth] for d in range(RING)]
    arrived = [turn(blocks[2], False, 2), turn(blocks[1], False, 1)]
    arrived += [turn(blocks[3], False, 3)]
    stage = add_up([blocks[0]] + arrived).astype(BF16)
    depth = stage.shape[0] // RING
    shares = [lax.dynamic_slice_in_dim(stage, ((zl + d) % RING) * depth, depth, axis=0) for d in range(RING)]
    input_grad = add_up(shares[:1] + [shift(shares[d], "zl", d) for d in range(1, RING)]).astype(BF16)
    return (hidden.T, input_grad.T, up_grad)


def solution(mesh):
    inner = Mesh(mesh.devices.reshape(RING, RING, RING, RING, 2), ("y", "x", "zl", "zh", "c"))
    tokens, features = ("zh", "c"), ("y", "x", "zl")
    return jax.shard_map(
        work,
        mesh=inner,
        in_specs=(P(tokens, features), P(tokens, features), P(features, None)),
        out_specs=(P(tokens, features), P(tokens, features), P(features, None)),
        check_vma=False,
    )
```

```python
import jax
import jax.numpy as jnp
from jax import lax
from jax.experimental import pallas as pl
from jax.experimental.pallas import tpu as pltpu
from jax.sharding import Mesh
from jax.sharding import PartitionSpec as P


inv_sqrt_two = 0.7071067811865476
inv_sqrt_two_pi = 0.3989422804014327


RING = 4
F32 = jnp.float32
BF16 = jnp.bfloat16


def gelu_parts(preact):
    normal_cdf = 0.5 * (1.0 + lax.erf(preact * inv_sqrt_two))
    gelu_out = preact * normal_cdf
    gelu_slope = normal_cdf + preact * jnp.exp(-0.5 * preact * preact) * inv_sqrt_two_pi
    return (gelu_out, gelu_slope)


def shift(value, axis, by):
    size = lax.axis_size(axis)
    return lax.ppermute(value, axis, [(i, (i + by) % size) for i in range(size)])


def dot(left, right, dims):
    return lax.dot_general(left, right, (dims, ((), ())), preferred_element_type=F32)


def spot_of(pos_ref, outer, inner):
    core = pos_ref[2]
    dy = outer + core * (inner - outer)
    dx = inner + core * (outer - inner)
    return lax.rem(pos_ref[0] + dy, RING), lax.rem(pos_ref[1] + dx, RING)


def column_of(pos_ref, outer, inner, width):
    y, x = spot_of(pos_ref, outer, inner)
    return pl.multiple_of((y * RING + x) * width, 128)


def order_kernel(pos_ref, up_ref, out_ref):
    width = up_ref.shape[1] // (RING * RING)
    for outer in range(RING):
        for inner in range(RING):
            out_ref[:, pl.ds((outer * RING + inner) * width, width)] = up_ref[
                :, pl.ds(column_of(pos_ref, outer, inner, width), width)
            ]


def early_kernel(up_ref, *refs):
    total_ref = refs[-1]
    depth = refs[0].shape[0]
    total = None
    for place, ref in zip((0, 1, 2, 3, 6, 7), refs[:-1]):
        term = dot(up_ref[:, pl.ds(place * depth, depth)], ref[...], ((1,), (0,)))
        total = term if total is None else total + term
    total_ref[...] = total


def forward_kernel(pos_ref, *refs):
    pieces = refs[0 : 2 * RING]
    early_ref, cot_ref, up_ref, hidden_ref, grad_ref, keep_ref, send_ref, packed_ref, term_ref = refs[2 * RING :]
    depth = pieces[0].shape[0]
    width = depth // 2
    rows = keep_ref.shape[1]
    total = early_ref[...]
    for place in (4, 5):
        total += dot(up_ref[:, pl.ds(place * depth, depth)], pieces[place][...], ((1,), (0,)))
    gelu_out, gelu_slope = gelu_parts(total)
    hidden_ref[...] = gelu_out.astype(BF16)
    grad_ref[...] = (cot_ref[...].astype(F32) * gelu_slope).astype(BF16)
    core, zh = pos_ref[2], pos_ref[3]
    for at, half in enumerate((core, 1 - core)):
        packed_ref[pl.ds(at * rows, rows), :] = grad_ref[pl.ds(pl.multiple_of(half * rows, 16), rows), :]
    grads = packed_ref[...]
    for place, piece in enumerate(pieces):
        term = dot(grads, piece[...], ((1,), (1,))).astype(BF16)
        for part in range(2):
            block = 2 * place + part
            y, x = spot_of(pos_ref, block // RING, block % RING)
            quarter = lax.rem(y + RING - zh, RING)
            where = pl.ds(pl.multiple_of(x * width, 128), width)
            for at in range(2):
                term_ref[at, quarter, :, where] = term[at * rows : (at + 1) * rows, part * width : (part + 1) * width]
    near, away = 1 + 2 * core, 3 - 2 * core
    for at, (half, quarter) in enumerate(((0, 2), (1, near), (0, near), (0, 0))):
        keep_ref[at] = term_ref[half, quarter]
    for at, (half, quarter) in enumerate(((1, 2), (0, away), (1, away), (1, 0))):
        send_ref[at] = term_ref[half, quarter]


def input_grad_kernel(grad_ref, up_ref, *outs):
    grads = grad_ref[...]
    depth = outs[0].shape[0]
    for d in range(2 * RING):
        term = dot(up_ref[:, pl.ds(d * depth, depth)], grads, ((0,), (0,)))
        outs[d][...] = term.astype(BF16)


def place_kernel(pos_ref, *refs):
    core, zh = pos_ref[2], pos_ref[3]
    pieces, (out_ref, whole_ref, sems) = refs[:8], refs[8:]
    rows, depth = pieces[0].shape
    behind, ahead = 3 - 2 * core, 1 + 2 * core
    halves = []
    for half, places in ((core, ((0, 0), (2, behind), (5, ahead), (6, 2))), (1 - core, ((1, 0), (3, behind), (4, ahead), (7, 2)))):
        where = pl.ds(pl.multiple_of(half * rows, 16), rows)
        copies = []
        for at, d in places:
            columns = pl.ds(pl.multiple_of(lax.rem(zh + d, RING) * depth, 128), depth)
            copies.append(pltpu.make_async_copy(pieces[at], whole_ref.at[where, columns], sems.at[at]))
            copies[-1].start()
        halves.append((where, copies))
    outs = []
    for at, (where, copies) in enumerate(halves):
        for copy in copies:
            copy.wait()
        outs.append(pltpu.make_async_copy(whole_ref.at[where, :], out_ref.at[where, :], sems.at[8 + at]))
        outs[-1].start()
    for copy in outs:
        copy.wait()


def vmem(count):
    return [pl.BlockSpec(memory_space=pltpu.VMEM)] * count


def turn(value, late, by):
    def target(y, x, c):
        if (c == 0) != late:
            return (y, (x + by) % RING, c)
        return ((y + by) % RING, x, c)

    def flat(y, x, c):
        return (y * RING + x) * 2 + c

    spots = [(y, x, c) for y in range(RING) for x in range(RING) for c in range(2)]
    return lax.ppermute(value, ("y", "x", "c"), [(flat(*s), flat(*target(*s))) for s in spots])


def advance(value, cross=False):
    pairs = []
    for zh in range(RING):
        pairs += [
            (zh * 2, (zh + 1) % RING * 2 + cross),
            (zh * 2 + 1, (zh - 1) % RING * 2 + 1 - cross),
        ]
    return lax.ppermute(value, ("zh", "c"), pairs)


def gather(value, late):
    return [value] + [turn(value, late, -d) for d in range(1, RING)]


def add_up(values):
    total = values[0].astype(F32)
    for value in values[1:]:
        total = total + value.astype(F32)
    return total


def work(normed, hidden_cot, up_rows):
    y, x, zl, zh, core = (lax.axis_index(a) for a in ("y", "x", "zl", "zh", "c"))
    pos = jnp.stack([y, x, core, zh]).astype(jnp.int32)
    hid, width = up_rows.shape
    tokens = normed.shape[0]
    scalars = pl.BlockSpec(memory_space=pltpu.SMEM)

    ordered = pl.pallas_call(
        order_kernel,
        in_specs=[scalars] + vmem(1),
        out_specs=vmem(1)[0],
        out_shape=jax.ShapeDtypeStruct((hid, width), BF16),
        name="order",
        cost_estimate=pl.CostEstimate(flops=0, bytes_accessed=4 * hid * width, transcendentals=0),
    )(pos, up_rows)

    share = normed.T
    shares = [share] + [shift(share, "zl", -d) for d in range(1, RING)]
    block = jnp.zeros((RING * share.shape[0], tokens), BF16)
    for d in range(RING):
        block = lax.dynamic_update_slice_in_dim(block, shares[d], (zl + d) % RING * share.shape[0], axis=0)
    quarters = gather(block, False)
    upper, lower = jnp.concatenate(quarters[:2], axis=0), jnp.concatenate(quarters[2:], axis=0)
    upper1, lower3 = turn(upper, True, -1), turn(lower, True, 1)
    lower1, upper3 = turn(lower, True, -1), turn(upper, True, 1)
    upper2, lower2 = turn(upper1, True, -1), turn(lower3, True, 1)
    pieces = [upper, lower, upper1, lower1, upper2, lower2, upper3, lower3]
    early = pl.pallas_call(
        early_kernel,
        in_specs=vmem(7),
        out_specs=vmem(1)[0],
        out_shape=jax.ShapeDtypeStruct((hid, tokens), F32),
        name="early",
        cost_estimate=pl.CostEstimate(flops=3 * hid * tokens * width // 2, bytes_accessed=7_000_000, transcendentals=0),
    )(ordered, *pieces[:4], *pieces[6:])

    hidden, hidden_grad, keep, send = pl.pallas_call(
        forward_kernel,
        in_specs=[scalars] + vmem(2 * RING + 3),
        out_specs=vmem(4),
        out_shape=[jax.ShapeDtypeStruct((hid, tokens), BF16)] * 2
        + [jax.ShapeDtypeStruct((4, hid // 2, width // RING), BF16)] * 2,
        scratch_shapes=[
            pltpu.VMEM((hid, tokens), BF16),
            pltpu.VMEM((2, RING, hid // 2, width // RING), BF16),
        ],
        name="forward",
        cost_estimate=pl.CostEstimate(
            flops=3 * hid * tokens * width, bytes_accessed=14_000_000, transcendentals=hid * tokens * 2
        ),
    )(pos, *pieces, early, hidden_cot.T, ordered)

    arrived = shift(send, "c", 1)
    opposite, follow, lead = (add_up([keep[at], arrived[at]]) for at in range(3))
    passed = advance(opposite.astype(BF16))
    cross_in = advance(follow.astype(BF16), cross=True)
    lead_in = advance((lead + passed.astype(F32)).astype(BF16))
    mine = (add_up([keep[3], arrived[3], cross_in, lead_in]) / (2 * RING)).astype(BF16)
    next_lead = advance(mine)
    other_mine = shift(mine, "c", 1)
    next_follow = advance(other_mine)
    far = advance(next_lead)
    other_next_lead = shift(next_lead, "c", 1)
    other_next_follow = shift(next_follow, "c", 1)
    other_far = shift(far, "c", 1)
    up_grad = pl.pallas_call(
        place_kernel,
        in_specs=[scalars] + [pl.BlockSpec(memory_space=pl.ANY)] * 8,
        out_specs=pl.BlockSpec(memory_space=pl.ANY),
        out_shape=jax.ShapeDtypeStruct((hid, width), BF16),
        scratch_shapes=[pltpu.VMEM((hid, width), BF16), pltpu.SemaphoreType.DMA((10,))],
        compiler_params=pltpu.CompilerParams(vmem_limit_bytes=8 << 20),
        name="place",
        cost_estimate=pl.CostEstimate(flops=0, bytes_accessed=4 * hid * width, transcendentals=0),
    )(pos, mine, other_mine, next_lead, next_follow, other_next_lead, other_next_follow, far, other_far)

    parts = pl.pallas_call(
        input_grad_kernel,
        in_specs=vmem(2),
        out_specs=vmem(2 * RING),
        out_shape=[jax.ShapeDtypeStruct((width // RING // 2, tokens), BF16)] * (2 * RING),
        name="partial",
        cost_estimate=pl.CostEstimate(
            flops=2 * hid * tokens * width, bytes_accessed=9_000_000, transcendentals=0
        ),
    )(hidden_grad, ordered)
    upper, lower = parts[0::2], parts[1::2]
    upper_in, lower_in = turn(upper[2], True, 1), turn(lower[2], True, -1)
    lower_left, upper_right = turn(lower[1], True, 1), turn(upper[3], True, -1)
    upper_left = turn(add_up([upper[1], upper_in]).astype(BF16), True, 1)
    lower_right = turn(add_up([lower[3], lower_in]).astype(BF16), True, -1)
    stage = jnp.concatenate(
        [
            add_up([upper[0], upper_left, upper_right]).astype(BF16),
            add_up([lower[0], lower_left, lower_right]).astype(BF16),
        ],
        axis=0,
    )
    depth = stage.shape[0] // RING
    blocks = [stage[d * depth : (d + 1) * depth] for d in range(RING)]
    arrived = [turn(blocks[2], False, 2), turn(blocks[1], False, 1)]
    arrived += [turn(blocks[3], False, 3)]
    stage = add_up([blocks[0]] + arrived).astype(BF16)
    depth = stage.shape[0] // RING
    shares = [lax.dynamic_slice_in_dim(stage, ((zl + d) % RING) * depth, depth, axis=0) for d in range(RING)]
    input_grad = add_up(shares[:1] + [shift(shares[d], "zl", d) for d in range(1, RING)]).astype(BF16)
    return (hidden.T, input_grad.T, up_grad)


def solution(mesh):
    inner = Mesh(mesh.devices.reshape(RING, RING, RING, RING, 2), ("y", "x", "zl", "zh", "c"))
    tokens, features = ("zh", "c"), ("y", "x", "zl")
    return jax.shard_map(
        work,
        mesh=inner,
        in_specs=(P(tokens, features), P(tokens, features), P(features, None)),
        out_specs=(P(tokens, features), P(tokens, features), P(features, None)),
        check_vma=False,
    )
```

```python
import jax
import jax.numpy as jnp
from jax import lax
from jax.experimental import pallas as pl
from jax.experimental.pallas import tpu as pltpu
from jax.sharding import Mesh
from jax.sharding import PartitionSpec as P


inv_sqrt_two = 0.7071067811865476
inv_sqrt_two_pi = 0.3989422804014327


RING = 4
F32 = jnp.float32
BF16 = jnp.bfloat16


def gelu_parts(preact):
    normal_cdf = 0.5 * (1.0 + lax.erf(preact * inv_sqrt_two))
    gelu_out = preact * normal_cdf
    gelu_slope = normal_cdf + preact * jnp.exp(-0.5 * preact * preact) * inv_sqrt_two_pi
    return (gelu_out, gelu_slope)


def shift(value, axis, by):
    size = lax.axis_size(axis)
    return lax.ppermute(value, axis, [(i, (i + by) % size) for i in range(size)])


def dot(left, right, dims):
    return lax.dot_general(left, right, (dims, ((), ())), preferred_element_type=F32)


def spot_of(pos_ref, outer, inner):
    core = pos_ref[2]
    dy = outer + core * (inner - outer)
    dx = inner + core * (outer - inner)
    return lax.rem(pos_ref[0] + dy, RING), lax.rem(pos_ref[1] + dx, RING)


def column_of(pos_ref, outer, inner, width):
    y, x = spot_of(pos_ref, outer, inner)
    return pl.multiple_of((y * RING + x) * width, 128)


def order_kernel(pos_ref, up_ref, out_ref):
    width = up_ref.shape[1] // (RING * RING)
    for outer in range(RING):
        for inner in range(RING):
            out_ref[:, pl.ds((outer * RING + inner) * width, width)] = up_ref[
                :, pl.ds(column_of(pos_ref, outer, inner, width), width)
            ]


def early_kernel(up_ref, *refs):
    total_ref = refs[-1]
    depth = refs[0].shape[0]
    total = None
    for place, ref in zip((0, 1, 2, 3, 6, 7), refs[:-1]):
        term = dot(up_ref[:, pl.ds(place * depth, depth)], ref[...], ((1,), (0,)))
        total = term if total is None else total + term
    total_ref[...] = total


def forward_kernel(pos_ref, *refs):
    pieces = refs[0 : 2 * RING]
    early_ref, cot_ref, up_ref, hidden_ref, grad_ref, keep_ref, send_ref, packed_ref, term_ref = refs[2 * RING :]
    depth = pieces[0].shape[0]
    width = depth // 2
    rows = keep_ref.shape[1]
    total = early_ref[...]
    for place in (4, 5):
        total += dot(up_ref[:, pl.ds(place * depth, depth)], pieces[place][...], ((1,), (0,)))
    gelu_out, gelu_slope = gelu_parts(total)
    hidden_ref[...] = gelu_out.astype(BF16)
    grad_ref[...] = (cot_ref[...].astype(F32) * gelu_slope).astype(BF16)
    core, zh = pos_ref[2], pos_ref[3]
    for at, half in enumerate((core, 1 - core)):
        packed_ref[pl.ds(at * rows, rows), :] = grad_ref[pl.ds(pl.multiple_of(half * rows, 16), rows), :]
    grads = packed_ref[...]
    for place, piece in enumerate(pieces):
        term = dot(grads, piece[...], ((1,), (1,))).astype(BF16)
        for part in range(2):
            block = 2 * place + part
            y, x = spot_of(pos_ref, block // RING, block % RING)
            quarter = lax.rem(y + RING - zh, RING)
            where = pl.ds(pl.multiple_of(x * width, 128), width)
            for at in range(2):
                term_ref[at, quarter, :, where] = term[at * rows : (at + 1) * rows, part * width : (part + 1) * width]
    near, away = 1 + 2 * core, 3 - 2 * core
    for at, (half, quarter) in enumerate(((0, 2), (1, near), (0, near), (0, 0))):
        keep_ref[at] = term_ref[half, quarter]
    for at, (half, quarter) in enumerate(((1, 2), (0, away), (1, away), (1, 0))):
        send_ref[at] = term_ref[half, quarter]


def input_grad_kernel(grad_ref, up_ref, *outs):
    grads = grad_ref[...]
    depth = outs[0].shape[0]
    for d in range(2 * RING):
        term = dot(up_ref[:, pl.ds(d * depth, depth)], grads, ((0,), (0,)))
        outs[d][...] = term.astype(BF16)


def place_kernel(pos_ref, *refs):
    core, zh = pos_ref[2], pos_ref[3]
    pieces, (out_ref, whole_ref, sems) = refs[:8], refs[8:]
    rows, depth = pieces[0].shape
    behind, ahead = 3 - 2 * core, 1 + 2 * core
    halves = []
    for half, places in ((core, ((0, 0), (2, behind), (3, ahead), (6, 2))), (1 - core, ((1, 0), (4, ahead), (5, behind), (7, 2)))):
        where = pl.ds(pl.multiple_of(half * rows, 16), rows)
        copies = []
        for at, d in places:
            columns = pl.ds(pl.multiple_of(lax.rem(zh + d, RING) * depth, 128), depth)
            copies.append(pltpu.make_async_copy(pieces[at], whole_ref.at[where, columns], sems.at[at]))
            copies[-1].start()
        halves.append((where, copies))
    outs = []
    for at, (where, copies) in enumerate(halves):
        for copy in copies:
            copy.wait()
        outs.append(pltpu.make_async_copy(whole_ref.at[where, :], out_ref.at[where, :], sems.at[8 + at]))
        outs[-1].start()
    for copy in outs:
        copy.wait()


def vmem(count):
    return [pl.BlockSpec(memory_space=pltpu.VMEM)] * count


def turn(value, late, by):
    def target(y, x, c):
        if (c == 0) != late:
            return (y, (x + by) % RING, c)
        return ((y + by) % RING, x, c)

    def flat(y, x, c):
        return (y * RING + x) * 2 + c

    spots = [(y, x, c) for y in range(RING) for x in range(RING) for c in range(2)]
    return lax.ppermute(value, ("y", "x", "c"), [(flat(*s), flat(*target(*s))) for s in spots])


def advance(value, cross=False, back=False):
    pairs = []
    for zh in range(RING):
        up, down = (zh + 1) % RING * 2, (zh - 1) % RING * 2
        if back:
            up, down = down, up
        pairs += [(zh * 2, up + cross), (zh * 2 + 1, down + 1 - cross)]
    return lax.ppermute(value, ("zh", "c"), pairs)


def gather(value, late):
    return [value] + [turn(value, late, -d) for d in range(1, RING)]


def add_up(values):
    total = values[0].astype(F32)
    for value in values[1:]:
        total = total + value.astype(F32)
    return total


def work(normed, hidden_cot, up_rows):
    y, x, zl, zh, core = (lax.axis_index(a) for a in ("y", "x", "zl", "zh", "c"))
    pos = jnp.stack([y, x, core, zh]).astype(jnp.int32)
    hid, width = up_rows.shape
    tokens = normed.shape[0]
    scalars = pl.BlockSpec(memory_space=pltpu.SMEM)

    ordered = pl.pallas_call(
        order_kernel,
        in_specs=[scalars] + vmem(1),
        out_specs=vmem(1)[0],
        out_shape=jax.ShapeDtypeStruct((hid, width), BF16),
        name="order",
        cost_estimate=pl.CostEstimate(flops=0, bytes_accessed=4 * hid * width, transcendentals=0),
    )(pos, up_rows)

    share = normed.T
    shares = [share] + [shift(share, "zl", -d) for d in range(1, RING)]
    block = jnp.zeros((RING * share.shape[0], tokens), BF16)
    for d in range(RING):
        block = lax.dynamic_update_slice_in_dim(block, shares[d], (zl + d) % RING * share.shape[0], axis=0)
    quarters = gather(block, False)
    upper, lower = jnp.concatenate(quarters[:2], axis=0), jnp.concatenate(quarters[2:], axis=0)
    upper1, lower3 = turn(upper, True, -1), turn(lower, True, 1)
    lower1, upper3 = turn(lower, True, -1), turn(upper, True, 1)
    upper2, lower2 = turn(upper1, True, -1), turn(lower3, True, 1)
    pieces = [upper, lower, upper1, lower1, upper2, lower2, upper3, lower3]
    early = pl.pallas_call(
        early_kernel,
        in_specs=vmem(7),
        out_specs=vmem(1)[0],
        out_shape=jax.ShapeDtypeStruct((hid, tokens), F32),
        name="early",
        cost_estimate=pl.CostEstimate(flops=3 * hid * tokens * width // 2, bytes_accessed=7_000_000, transcendentals=0),
    )(ordered, *pieces[:4], *pieces[6:])

    hidden, hidden_grad, keep, send = pl.pallas_call(
        forward_kernel,
        in_specs=[scalars] + vmem(2 * RING + 3),
        out_specs=vmem(4),
        out_shape=[jax.ShapeDtypeStruct((hid, tokens), BF16)] * 2
        + [jax.ShapeDtypeStruct((4, hid // 2, width // RING), BF16)] * 2,
        scratch_shapes=[
            pltpu.VMEM((hid, tokens), BF16),
            pltpu.VMEM((2, RING, hid // 2, width // RING), BF16),
        ],
        name="forward",
        cost_estimate=pl.CostEstimate(
            flops=3 * hid * tokens * width, bytes_accessed=14_000_000, transcendentals=hid * tokens * 2
        ),
    )(pos, *pieces, early, hidden_cot.T, ordered)

    arrived = shift(send, "c", 1)
    opposite, follow, lead = (add_up([keep[at], arrived[at]]) for at in range(3))
    passed = advance(opposite.astype(BF16))
    cross_in = advance(follow.astype(BF16), cross=True)
    lead_in = advance((lead + passed.astype(F32)).astype(BF16))
    mine = (add_up([keep[3], arrived[3], cross_in, lead_in]) / (2 * RING)).astype(BF16)
    behind = advance(mine)
    ahead = advance(mine, back=True)
    far = advance(behind)
    swapped = []
    for value in (mine, behind, ahead, far):
        swapped.append(shift(value, "c", 1))
    up_grad = pl.pallas_call(
        place_kernel,
        in_specs=[scalars] + [pl.BlockSpec(memory_space=pl.ANY)] * 8,
        out_specs=pl.BlockSpec(memory_space=pl.ANY),
        out_shape=jax.ShapeDtypeStruct((hid, width), BF16),
        scratch_shapes=[pltpu.VMEM((hid, width), BF16), pltpu.SemaphoreType.DMA((10,))],
        compiler_params=pltpu.CompilerParams(vmem_limit_bytes=8 << 20),
        name="place",
        cost_estimate=pl.CostEstimate(flops=0, bytes_accessed=4 * hid * width, transcendentals=0),
    )(pos, mine, swapped[0], behind, ahead, swapped[1], swapped[2], far, swapped[3])

    parts = pl.pallas_call(
        input_grad_kernel,
        in_specs=vmem(2),
        out_specs=vmem(2 * RING),
        out_shape=[jax.ShapeDtypeStruct((width // RING // 2, tokens), BF16)] * (2 * RING),
        name="partial",
        cost_estimate=pl.CostEstimate(
            flops=2 * hid * tokens * width, bytes_accessed=9_000_000, transcendentals=0
        ),
    )(hidden_grad, ordered)
    upper, lower = parts[0::2], parts[1::2]
    upper_in, lower_in = turn(upper[2], True, 1), turn(lower[2], True, -1)
    lower_left, upper_right = turn(lower[1], True, 1), turn(upper[3], True, -1)
    upper_left = turn(add_up([upper[1], upper_in]).astype(BF16), True, 1)
    lower_right = turn(add_up([lower[3], lower_in]).astype(BF16), True, -1)
    stage = jnp.concatenate(
        [
            add_up([upper[0], upper_left, upper_right]).astype(BF16),
            add_up([lower[0], lower_left, lower_right]).astype(BF16),
        ],
        axis=0,
    )
    depth = stage.shape[0] // RING
    blocks = [stage[d * depth : (d + 1) * depth] for d in range(RING)]
    arrived = [turn(blocks[d], False, d) for d in range(1, RING)]
    stage = add_up([blocks[0]] + arrived).astype(BF16)
    depth = stage.shape[0] // RING
    shares = [lax.dynamic_slice_in_dim(stage, ((zl + d) % RING) * depth, depth, axis=0) for d in range(RING)]
    input_grad = add_up(shares[:1] + [shift(shares[d], "zl", d) for d in range(1, RING)]).astype(BF16)
    return (hidden.T, input_grad.T, up_grad)


def solution(mesh):
    inner = Mesh(mesh.devices.reshape(RING, RING, RING, RING, 2), ("y", "x", "zl", "zh", "c"))
    tokens, features = ("zh", "c"), ("y", "x", "zl")
    return jax.shard_map(
        work,
        mesh=inner,
        in_specs=(P(tokens, features), P(tokens, features), P(features, None)),
        out_specs=(P(tokens, features), P(tokens, features), P(features, None)),
        check_vma=False,
    )
```

```python
import jax
import jax.numpy as jnp
from jax import lax
from jax.experimental import pallas as pl
from jax.experimental.pallas import tpu as pltpu
from jax.sharding import Mesh
from jax.sharding import PartitionSpec as P


inv_sqrt_two = 0.7071067811865476
inv_sqrt_two_pi = 0.3989422804014327


RING = 4
F32 = jnp.float32
BF16 = jnp.bfloat16


def gelu_parts(preact):
    normal_cdf = 0.5 * (1.0 + lax.erf(preact * inv_sqrt_two))
    gelu_out = preact * normal_cdf
    gelu_slope = normal_cdf + preact * jnp.exp(-0.5 * preact * preact) * inv_sqrt_two_pi
    return (gelu_out, gelu_slope)


def shift(value, axis, by):
    size = lax.axis_size(axis)
    return lax.ppermute(value, axis, [(i, (i + by) % size) for i in range(size)])


def dot(left, right, dims):
    return lax.dot_general(left, right, (dims, ((), ())), preferred_element_type=F32)


def spot_of(pos_ref, outer, inner):
    core = pos_ref[2]
    dy = outer + core * (inner - outer)
    dx = inner + core * (outer - inner)
    return lax.rem(pos_ref[0] + dy, RING), lax.rem(pos_ref[1] + dx, RING)


def column_of(pos_ref, outer, inner, width):
    y, x = spot_of(pos_ref, outer, inner)
    return pl.multiple_of((y * RING + x) * width, 128)


def order_kernel(pos_ref, up_ref, out_ref):
    width = up_ref.shape[1] // (RING * RING)
    for outer in range(RING):
        for inner in range(RING):
            out_ref[:, pl.ds((outer * RING + inner) * width, width)] = up_ref[
                :, pl.ds(column_of(pos_ref, outer, inner, width), width)
            ]


def early_kernel(up_ref, *refs):
    total_ref = refs[-1]
    depth = refs[0].shape[0]
    total = None
    for place, ref in zip((0, 1, 2, 3, 6, 7), refs[:-1]):
        term = dot(up_ref[:, pl.ds(place * depth, depth)], ref[...], ((1,), (0,)))
        total = term if total is None else total + term
    total_ref[...] = total


def forward_kernel(pos_ref, *refs):
    pieces = refs[0 : 2 * RING]
    early_ref, cot_ref, up_ref, hidden_ref, grad_ref, keep_ref, send_ref, packed_ref, term_ref = refs[2 * RING :]
    depth = pieces[0].shape[0]
    width = depth // 2
    rows = keep_ref.shape[1]
    total = early_ref[...]
    for place in (4, 5):
        total += dot(up_ref[:, pl.ds(place * depth, depth)], pieces[place][...], ((1,), (0,)))
    gelu_out, gelu_slope = gelu_parts(total)
    hidden_ref[...] = gelu_out.astype(BF16)
    grad_ref[...] = (cot_ref[...].astype(F32) * gelu_slope).astype(BF16)
    core, zh = pos_ref[2], pos_ref[3]
    for at, half in enumerate((core, 1 - core)):
        packed_ref[pl.ds(at * rows, rows), :] = grad_ref[pl.ds(pl.multiple_of(half * rows, 16), rows), :]
    grads = packed_ref[...]
    for place, piece in enumerate(pieces):
        term = dot(grads, piece[...], ((1,), (1,))).astype(BF16)
        for part in range(2):
            block = 2 * place + part
            y, x = spot_of(pos_ref, block // RING, block % RING)
            quarter = lax.rem(y + RING - zh, RING)
            where = pl.ds(pl.multiple_of(x * width, 128), width)
            for at in range(2):
                term_ref[at, quarter, :, where] = term[at * rows : (at + 1) * rows, part * width : (part + 1) * width]
    near, away = 1 + 2 * core, 3 - 2 * core
    for at, (half, quarter) in enumerate(((0, 2), (1, near), (0, near), (0, 0))):
        keep_ref[at] = term_ref[half, quarter]
    for at, (half, quarter) in enumerate(((1, 2), (0, away), (1, away), (1, 0))):
        send_ref[at] = term_ref[half, quarter]


def input_grad_kernel(grad_ref, up_ref, *outs):
    grads = grad_ref[...]
    depth = outs[0].shape[0]
    for d in range(2 * RING):
        term = dot(up_ref[:, pl.ds(d * depth, depth)], grads, ((0,), (0,)))
        outs[d][...] = term.astype(BF16)


def place_kernel(pos_ref, *refs):
    core, zh = pos_ref[2], pos_ref[3]
    pieces, (out_ref, whole_ref, sems) = refs[:8], refs[8:]
    rows, depth = pieces[0].shape
    behind, ahead = 3 - 2 * core, 1 + 2 * core
    halves = []
    for half, places in ((core, ((0, 0), (2, behind), (3, ahead), (6, 2))), (1 - core, ((1, 0), (4, ahead), (5, behind), (7, 2)))):
        where = pl.ds(pl.multiple_of(half * rows, 16), rows)
        copies = []
        for at, d in places:
            columns = pl.ds(pl.multiple_of(lax.rem(zh + d, RING) * depth, 128), depth)
            copies.append(pltpu.make_async_copy(pieces[at], whole_ref.at[where, columns], sems.at[at]))
            copies[-1].start()
        halves.append((where, copies))
    outs = []
    for at, (where, copies) in enumerate(halves):
        for copy in copies:
            copy.wait()
        outs.append(pltpu.make_async_copy(whole_ref.at[where, :], out_ref.at[where, :], sems.at[8 + at]))
        outs[-1].start()
    for copy in outs:
        copy.wait()


def vmem(count):
    return [pl.BlockSpec(memory_space=pltpu.VMEM)] * count


def turn(value, late, by):
    def target(y, x, c):
        if (c == 0) != late:
            return (y, (x + by) % RING, c)
        return ((y + by) % RING, x, c)

    def flat(y, x, c):
        return (y * RING + x) * 2 + c

    spots = [(y, x, c) for y in range(RING) for x in range(RING) for c in range(2)]
    return lax.ppermute(value, ("y", "x", "c"), [(flat(*s), flat(*target(*s))) for s in spots])


def advance(value, cross=False, back=False):
    pairs = []
    for zh in range(RING):
        up, down = (zh + 1) % RING * 2, (zh - 1) % RING * 2
        if back:
            up, down = down, up
        pairs += [(zh * 2, up + cross), (zh * 2 + 1, down + 1 - cross)]
    return lax.ppermute(value, ("zh", "c"), pairs)


def gather(value, late):
    return [value] + [turn(value, late, -d) for d in range(1, RING)]


def add_up(values):
    total = values[0].astype(F32)
    for value in values[1:]:
        total = total + value.astype(F32)
    return total


def work(normed, hidden_cot, up_rows):
    y, x, zl, zh, core = (lax.axis_index(a) for a in ("y", "x", "zl", "zh", "c"))
    pos = jnp.stack([y, x, core, zh]).astype(jnp.int32)
    hid, width = up_rows.shape
    tokens = normed.shape[0]
    scalars = pl.BlockSpec(memory_space=pltpu.SMEM)

    ordered = pl.pallas_call(
        order_kernel,
        in_specs=[scalars] + vmem(1),
        out_specs=vmem(1)[0],
        out_shape=jax.ShapeDtypeStruct((hid, width), BF16),
        name="order",
        cost_estimate=pl.CostEstimate(flops=0, bytes_accessed=4 * hid * width, transcendentals=0),
    )(pos, up_rows)

    share = normed.T
    shares = [share] + [shift(share, "zl", -d) for d in range(1, RING)]
    block = jnp.zeros((RING * share.shape[0], tokens), BF16)
    for d in range(RING):
        block = lax.dynamic_update_slice_in_dim(block, shares[d], (zl + d) % RING * share.shape[0], axis=0)
    quarters = gather(block, False)
    upper, lower = jnp.concatenate(quarters[:2], axis=0), jnp.concatenate(quarters[2:], axis=0)
    upper1, lower3 = turn(upper, True, -1), turn(lower, True, 1)
    lower1, upper3 = turn(lower, True, -1), turn(upper, True, 1)
    upper2, lower2 = turn(upper1, True, -1), turn(lower3, True, 1)
    pieces = [upper, lower, upper1, lower1, upper2, lower2, upper3, lower3]
    early = pl.pallas_call(
        early_kernel,
        in_specs=vmem(7),
        out_specs=vmem(1)[0],
        out_shape=jax.ShapeDtypeStruct((hid, tokens), F32),
        name="early",
        cost_estimate=pl.CostEstimate(flops=3 * hid * tokens * width // 2, bytes_accessed=7_000_000, transcendentals=0),
    )(ordered, *pieces[:4], *pieces[6:])

    hidden, hidden_grad, keep, send = pl.pallas_call(
        forward_kernel,
        in_specs=[scalars] + vmem(2 * RING + 3),
        out_specs=vmem(4),
        out_shape=[jax.ShapeDtypeStruct((hid, tokens), BF16)] * 2
        + [jax.ShapeDtypeStruct((4, hid // 2, width // RING), BF16)] * 2,
        scratch_shapes=[
            pltpu.VMEM((hid, tokens), BF16),
            pltpu.VMEM((2, RING, hid // 2, width // RING), BF16),
        ],
        name="forward",
        cost_estimate=pl.CostEstimate(
            flops=3 * hid * tokens * width, bytes_accessed=14_000_000, transcendentals=hid * tokens * 2
        ),
    )(pos, *pieces, early, hidden_cot.T, ordered)

    arrived = shift(send, "c", 1)
    opposite, follow, lead = (add_up([keep[at], arrived[at]]) for at in range(3))
    passed = advance(opposite.astype(BF16))
    cross_in = advance(follow.astype(BF16), cross=True)
    lead_in = advance((lead + passed.astype(F32)).astype(BF16))
    mine = (add_up([keep[3], arrived[3], cross_in, lead_in]) / (2 * RING)).astype(BF16)
    behind = advance(mine)
    ahead = advance(mine, back=True)
    far = advance(behind)
    swapped = []
    for value in (mine, behind, ahead, far):
        swapped.append(shift(value, "c", 1))
    up_grad = pl.pallas_call(
        place_kernel,
        in_specs=[scalars] + [pl.BlockSpec(memory_space=pl.ANY)] * 8,
        out_specs=pl.BlockSpec(memory_space=pl.ANY),
        out_shape=jax.ShapeDtypeStruct((hid, width), BF16),
        scratch_shapes=[pltpu.VMEM((hid, width), BF16), pltpu.SemaphoreType.DMA((10,))],
        compiler_params=pltpu.CompilerParams(vmem_limit_bytes=8 << 20),
        name="place",
        cost_estimate=pl.CostEstimate(flops=0, bytes_accessed=4 * hid * width, transcendentals=0),
    )(pos, mine, swapped[0], behind, ahead, swapped[1], swapped[2], far, swapped[3])

    parts = pl.pallas_call(
        input_grad_kernel,
        in_specs=vmem(2),
        out_specs=vmem(2 * RING),
        out_shape=[jax.ShapeDtypeStruct((width // RING // 2, tokens), BF16)] * (2 * RING),
        name="partial",
        cost_estimate=pl.CostEstimate(
            flops=2 * hid * tokens * width, bytes_accessed=9_000_000, transcendentals=0
        ),
    )(hidden_grad, ordered)
    upper, lower = parts[0::2], parts[1::2]
    upper_in, lower_in = turn(upper[2], True, 1), turn(lower[2], True, -1)
    lower_left, upper_right = turn(lower[1], True, 1), turn(upper[3], True, -1)
    upper_left = turn(add_up([upper[1], upper_in]).astype(BF16), True, 1)
    lower_right = turn(add_up([lower[3], lower_in]).astype(BF16), True, -1)
    stage = jnp.concatenate(
        [
            add_up([upper[0], upper_left, upper_right]).astype(BF16),
            add_up([lower[0], lower_left, lower_right]).astype(BF16),
        ],
        axis=0,
    )
    depth = stage.shape[0] // RING
    blocks = [stage[d * depth : (d + 1) * depth] for d in range(RING)]
    arrived = [turn(blocks[2], False, 2), turn(blocks[1], False, 1)]
    arrived += [turn(blocks[3], False, 3)]
    stage = add_up([blocks[0]] + arrived).astype(BF16)
    depth = stage.shape[0] // RING
    shares = [lax.dynamic_slice_in_dim(stage, ((zl + d) % RING) * depth, depth, axis=0) for d in range(RING)]
    arrived = [shift(shares[d], "zl", d) for d in range(1, RING)]
    up_grad, *arrived = lax.optimization_barrier([up_grad, *arrived])
    input_grad = add_up(shares[:1] + arrived).astype(BF16)
    return (hidden.T, input_grad.T, up_grad)


def solution(mesh):
    inner = Mesh(mesh.devices.reshape(RING, RING, RING, RING, 2), ("y", "x", "zl", "zh", "c"))
    tokens, features = ("zh", "c"), ("y", "x", "zl")
    return jax.shard_map(
        work,
        mesh=inner,
        in_specs=(P(tokens, features), P(tokens, features), P(features, None)),
        out_specs=(P(tokens, features), P(tokens, features), P(features, None)),
        check_vma=False,
    )
```

```python
import jax
import jax.numpy as jnp
from jax import lax
from jax.experimental import pallas as pl
from jax.experimental.pallas import tpu as pltpu
from jax.sharding import Mesh
from jax.sharding import PartitionSpec as P


inv_sqrt_two = 0.7071067811865476
inv_sqrt_two_pi = 0.3989422804014327


RING = 4
F32 = jnp.float32
BF16 = jnp.bfloat16


def gelu_parts(preact):
    normal_cdf = 0.5 * (1.0 + lax.erf(preact * inv_sqrt_two))
    gelu_out = preact * normal_cdf
    gelu_slope = normal_cdf + preact * jnp.exp(-0.5 * preact * preact) * inv_sqrt_two_pi
    return (gelu_out, gelu_slope)


def shift(value, axis, by):
    size = lax.axis_size(axis)
    return lax.ppermute(value, axis, [(i, (i + by) % size) for i in range(size)])


def dot(left, right, dims):
    return lax.dot_general(left, right, (dims, ((), ())), preferred_element_type=F32)


def spot_of(pos_ref, outer, inner):
    core = pos_ref[2]
    dy = outer + core * (inner - outer)
    dx = inner + core * (outer - inner)
    return lax.rem(pos_ref[0] + dy, RING), lax.rem(pos_ref[1] + dx, RING)


def column_of(pos_ref, outer, inner, width):
    y, x = spot_of(pos_ref, outer, inner)
    return pl.multiple_of((y * RING + x) * width, 128)


def order_kernel(pos_ref, up_ref, out_ref):
    width = up_ref.shape[1] // (RING * RING)
    for outer in range(RING):
        for inner in range(RING):
            out_ref[:, pl.ds((outer * RING + inner) * width, width)] = up_ref[
                :, pl.ds(column_of(pos_ref, outer, inner, width), width)
            ]


def early_kernel(up_ref, *refs):
    total_ref = refs[-1]
    depth = refs[0].shape[0]
    total = None
    for place, ref in zip((0, 1, 2, 3, 6, 7), refs[:-1]):
        term = dot(up_ref[:, pl.ds(place * depth, depth)], ref[...], ((1,), (0,)))
        total = term if total is None else total + term
    total_ref[...] = total


def forward_kernel(pos_ref, *refs):
    pieces = refs[0 : 2 * RING]
    early_ref, cot_ref, up_ref, hidden_ref, grad_ref, keep_ref, send_ref, packed_ref, term_ref = refs[2 * RING :]
    depth = pieces[0].shape[0]
    width = depth // 2
    rows = keep_ref.shape[1]
    total = early_ref[...]
    for place in (4, 5):
        total += dot(up_ref[:, pl.ds(place * depth, depth)], pieces[place][...], ((1,), (0,)))
    gelu_out, gelu_slope = gelu_parts(total)
    hidden_ref[...] = gelu_out.astype(BF16)
    grad_ref[...] = (cot_ref[...].astype(F32) * gelu_slope).astype(BF16)
    core, zh = pos_ref[2], pos_ref[3]
    for at, half in enumerate((core, 1 - core)):
        packed_ref[pl.ds(at * rows, rows), :] = grad_ref[pl.ds(pl.multiple_of(half * rows, 16), rows), :]
    grads = packed_ref[...]
    for place, piece in enumerate(pieces):
        term = dot(grads, piece[...], ((1,), (1,))).astype(BF16)
        for part in range(2):
            block = 2 * place + part
            y, x = spot_of(pos_ref, block // RING, block % RING)
            quarter = lax.rem(y + RING - zh, RING)
            where = pl.ds(pl.multiple_of(x * width, 128), width)
            for at in range(2):
                term_ref[at, quarter, :, where] = term[at * rows : (at + 1) * rows, part * width : (part + 1) * width]
    near, away = 1 + 2 * core, 3 - 2 * core
    for at, (half, quarter) in enumerate(((0, 2), (1, near), (0, near), (0, 0))):
        keep_ref[at] = term_ref[half, quarter]
    for at, (half, quarter) in enumerate(((1, 2), (0, away), (1, away), (1, 0))):
        send_ref[at] = term_ref[half, quarter]


def input_grad_kernel(grad_ref, up_ref, *outs):
    grads = grad_ref[...]
    depth = outs[0].shape[0]
    for d in range(2 * RING):
        term = dot(up_ref[:, pl.ds(d * depth, depth)], grads, ((0,), (0,)))
        outs[d][...] = term.astype(BF16)


def place_kernel(pos_ref, *refs):
    core, zh = pos_ref[2], pos_ref[3]
    own, (packed_ref, other_far_ref, out_ref, whole_ref, sems) = refs[:4], refs[4:]
    rows, depth = own[0].shape
    others = [packed_ref.at[:, pl.ds(at * depth, depth)] for at in range(3)] + [other_far_ref]
    behind, ahead = 3 - 2 * core, 1 + 2 * core
    halves = []
    for half, pieces, places in ((core, own, (0, behind, ahead, 2)), (1 - core, others, (0, ahead, behind, 2))):
        where = pl.ds(pl.multiple_of(half * rows, 16), rows)
        copies = []
        for at, d in enumerate(places):
            columns = pl.ds(pl.multiple_of(lax.rem(zh + d, RING) * depth, 128), depth)
            copies.append(pltpu.make_async_copy(pieces[at], whole_ref.at[where, columns], sems.at[len(halves), at]))
            copies[-1].start()
        halves.append((where, copies))
    outs = []
    for at, (where, copies) in enumerate(halves):
        for copy in copies:
            copy.wait()
        outs.append(pltpu.make_async_copy(whole_ref.at[where, :], out_ref.at[where, :], sems.at[at, RING]))
        outs[-1].start()
    for copy in outs:
        copy.wait()


def vmem(count):
    return [pl.BlockSpec(memory_space=pltpu.VMEM)] * count


def turn(value, late, by):
    def target(y, x, c):
        if (c == 0) != late:
            return (y, (x + by) % RING, c)
        return ((y + by) % RING, x, c)

    def flat(y, x, c):
        return (y * RING + x) * 2 + c

    spots = [(y, x, c) for y in range(RING) for x in range(RING) for c in range(2)]
    return lax.ppermute(value, ("y", "x", "c"), [(flat(*s), flat(*target(*s))) for s in spots])


def advance(value, cross=False, back=False):
    pairs = []
    for zh in range(RING):
        up, down = (zh + 1) % RING * 2, (zh - 1) % RING * 2
        if back:
            up, down = down, up
        pairs += [(zh * 2, up + cross), (zh * 2 + 1, down + 1 - cross)]
    return lax.ppermute(value, ("zh", "c"), pairs)


def gather(value, late):
    return [value] + [turn(value, late, -d) for d in range(1, RING)]


def add_up(values):
    total = values[0].astype(F32)
    for value in values[1:]:
        total = total + value.astype(F32)
    return total


def work(normed, hidden_cot, up_rows):
    y, x, zl, zh, core = (lax.axis_index(a) for a in ("y", "x", "zl", "zh", "c"))
    pos = jnp.stack([y, x, core, zh]).astype(jnp.int32)
    hid, width = up_rows.shape
    tokens = normed.shape[0]
    scalars = pl.BlockSpec(memory_space=pltpu.SMEM)

    ordered = pl.pallas_call(
        order_kernel,
        in_specs=[scalars] + vmem(1),
        out_specs=vmem(1)[0],
        out_shape=jax.ShapeDtypeStruct((hid, width), BF16),
        name="order",
        cost_estimate=pl.CostEstimate(flops=0, bytes_accessed=4 * hid * width, transcendentals=0),
    )(pos, up_rows)

    share = normed.T
    shares = [share] + [shift(share, "zl", -d) for d in range(1, RING)]
    block = jnp.zeros((RING * share.shape[0], tokens), BF16)
    for d in range(RING):
        block = lax.dynamic_update_slice_in_dim(block, shares[d], (zl + d) % RING * share.shape[0], axis=0)
    quarters = gather(block, False)
    upper, lower = jnp.concatenate(quarters[:2], axis=0), jnp.concatenate(quarters[2:], axis=0)
    upper1, lower3 = turn(upper, True, -1), turn(lower, True, 1)
    lower1, upper3 = turn(lower, True, -1), turn(upper, True, 1)
    upper2, lower2 = turn(upper1, True, -1), turn(lower3, True, 1)
    pieces = [upper, lower, upper1, lower1, upper2, lower2, upper3, lower3]
    early = pl.pallas_call(
        early_kernel,
        in_specs=vmem(7),
        out_specs=vmem(1)[0],
        out_shape=jax.ShapeDtypeStruct((hid, tokens), F32),
        name="early",
        cost_estimate=pl.CostEstimate(flops=3 * hid * tokens * width // 2, bytes_accessed=7_000_000, transcendentals=0),
    )(ordered, *pieces[:4], *pieces[6:])

    hidden, hidden_grad, keep, send = pl.pallas_call(
        forward_kernel,
        in_specs=[scalars] + vmem(2 * RING + 3),
        out_specs=vmem(4),
        out_shape=[jax.ShapeDtypeStruct((hid, tokens), BF16)] * 2
        + [jax.ShapeDtypeStruct((4, hid // 2, width // RING), BF16)] * 2,
        scratch_shapes=[
            pltpu.VMEM((hid, tokens), BF16),
            pltpu.VMEM((2, RING, hid // 2, width // RING), BF16),
        ],
        name="forward",
        cost_estimate=pl.CostEstimate(
            flops=3 * hid * tokens * width, bytes_accessed=14_000_000, transcendentals=hid * tokens * 2
        ),
    )(pos, *pieces, early, hidden_cot.T, ordered)

    arrived = shift(send, "c", 1)
    opposite, follow, lead = (add_up([keep[at], arrived[at]]) for at in range(3))
    passed = advance(opposite.astype(BF16))
    cross_in = advance(follow.astype(BF16), cross=True)
    lead_in = advance((lead + passed.astype(F32)).astype(BF16))
    mine = (add_up([keep[3], arrived[3], cross_in, lead_in]) / (2 * RING)).astype(BF16)
    behind = advance(mine)
    ahead = advance(mine, back=True)
    far = advance(behind)
    packed = jnp.concatenate([mine, behind, ahead], axis=1)
    other_packed = shift(packed, "c", 1)
    other_far = shift(far, "c", 1)
    up_grad = pl.pallas_call(
        place_kernel,
        in_specs=[scalars] + [pl.BlockSpec(memory_space=pl.ANY)] * 6,
        out_specs=pl.BlockSpec(memory_space=pl.ANY),
        out_shape=jax.ShapeDtypeStruct((hid, width), BF16),
        scratch_shapes=[pltpu.VMEM((hid, width), BF16), pltpu.SemaphoreType.DMA((2, RING + 1))],
        compiler_params=pltpu.CompilerParams(vmem_limit_bytes=8 << 20),
        name="place",
        cost_estimate=pl.CostEstimate(flops=0, bytes_accessed=4 * hid * width, transcendentals=0),
    )(pos, mine, behind, ahead, far, other_packed, other_far)

    parts = pl.pallas_call(
        input_grad_kernel,
        in_specs=vmem(2),
        out_specs=vmem(2 * RING),
        out_shape=[jax.ShapeDtypeStruct((width // RING // 2, tokens), BF16)] * (2 * RING),
        name="partial",
        cost_estimate=pl.CostEstimate(
            flops=2 * hid * tokens * width, bytes_accessed=9_000_000, transcendentals=0
        ),
    )(hidden_grad, ordered)
    upper, lower = parts[0::2], parts[1::2]
    upper_in, lower_in = turn(upper[2], True, 1), turn(lower[2], True, -1)
    lower_left, upper_right = turn(lower[1], True, 1), turn(upper[3], True, -1)
    upper_left = turn(add_up([upper[1], upper_in]).astype(BF16), True, 1)
    lower_right = turn(add_up([lower[3], lower_in]).astype(BF16), True, -1)
    stage = jnp.concatenate(
        [
            add_up([upper[0], upper_left, upper_right]).astype(BF16),
            add_up([lower[0], lower_left, lower_right]).astype(BF16),
        ],
        axis=0,
    )
    depth = stage.shape[0] // RING
    blocks = [stage[d * depth : (d + 1) * depth] for d in range(RING)]
    arrived = [turn(blocks[2], False, 2), turn(blocks[1], False, 1)]
    arrived += [turn(blocks[3], False, 3)]
    stage = add_up([blocks[0]] + arrived).astype(BF16)
    depth = stage.shape[0] // RING
    shares = [lax.dynamic_slice_in_dim(stage, ((zl + d) % RING) * depth, depth, axis=0) for d in range(RING)]
    arrived = [shift(shares[d], "zl", d) for d in range(1, RING)]
    up_grad, *arrived = lax.optimization_barrier([up_grad, *arrived])
    input_grad = add_up(shares[:1] + arrived).astype(BF16)
    return (hidden.T, input_grad.T, up_grad)


def solution(mesh):
    inner = Mesh(mesh.devices.reshape(RING, RING, RING, RING, 2), ("y", "x", "zl", "zh", "c"))
    tokens, features = ("zh", "c"), ("y", "x", "zl")
    return jax.shard_map(
        work,
        mesh=inner,
        in_specs=(P(tokens, features), P(tokens, features), P(features, None)),
        out_specs=(P(tokens, features), P(tokens, features), P(features, None)),
        check_vma=False,
    )
```
